32 devices in a mesh: groups: 2 (over x), seq: 8 (over z, y), head: 2 (over core).
Axes of the slice: x: 2, y: 2, z: 4, core: 2. Of those that a mesh axis runs over, the one named last changes fastest.
Arguments:
- queries: bfloat16 [512, 4096], P(('groups', 'seq'), 'head'), parts along dimension 0, may hold values from -24 to 24
- vision: bfloat16 [4096, 7680], P(('groups', 'seq')), parts along dimension 0, may hold values from -6 to 6
- key_matrix: bfloat16 [7680, 512], P('seq', 'head'), may hold values from -0.0625 to 0.0625
- value_matrix: bfloat16 [7680, 512], P('seq', 'head'), may hold values from -0.0625 to 0.0625
- out_weight: bfloat16 [4096, 8192], P('head', 'seq'), may hold values from -0.09375 to 0.09375
- residual: bfloat16 [512, 8192], P(('groups', 'head'), 'seq'), parts along dimension 0, may hold values from -4 to 4
- query_norm_gain: float32 [128], replicated, may hold values from 1 to 12
- key_norm_gain: float32 [128], replicated, may hold values from 1 to 12
- attn_gate: float32 [1], replicated, may hold values from 0.5 to 2
Outputs:
- mixed: bfloat16 [512, 8192], P(('groups', 'head'), 'seq'), parts along dimension 0
The draws below stay inside these ranges and needn't reach their ends.
There are 2 independent parts, one for each index of `groups`. The reference program is written for one: setup_inputs(seed, part) draws one part's arguments, and reference() takes and returns one part's arrays. A program takes and returns all parts, laid end to end along the dimension named above; an argument that names none is the same for every part. Nothing has to cross between parts.
All inputs are finite; a program needn't handle non-finite values.
Results may differ from the reference program's by a relative error of at most 0.015.
The reference program's roundings to bfloat16 on the way count: a program that leaves them out, or rounds other values in their place, can miss the bound.
Values may be sent and summed in bfloat16 or wider, within the bound.
A program may use at most 64 MiB of HBM per device.

```python
import math
import jax
import jax.numpy as jnp
from jax import lax

D = 8192
VISION_WIDTH = 7680
HEAD_SIZE = 128
QUERY_HEADS = 32
KEY_VALUE_HEADS = 4
TEXT_TOKENS = 256
VISION_TOKENS = 2048


def draw_queries(key, part):
    base = jax.random.normal(key, (TEXT_TOKENS, QUERY_HEADS * HEAD_SIZE), jnp.float32)
    return jnp.clip(base, -6.0, 6.0).astype(jnp.bfloat16)


def gain_values(key, salt):
    base = jnp.exp(jax.random.uniform(jax.random.fold_in(key, salt), (HEAD_SIZE,), jnp.float32, 0.0, math.log(3.0)))
    return base


def draw_query_norm_gain(key, part):
    return gain_values(key, 21)


def draw_key_norm_gain(key, part):
    return gain_values(key, 37)


def steps_of(stream_key, dims, cuts, low, largest):
    level, own = 1.0, jax.random.fold_in(stream_key, 6)
    for dim, blocks in cuts:
        draws = jnp.exp(jax.random.uniform(jax.random.fold_in(own, dim), (blocks,), jnp.float32, low / len(cuts), largest / len(cuts)))
        level = level * jnp.repeat(draws, dims[dim] // blocks).reshape([-1 if axis == dim else 1 for axis in range(len(dims))])
    return level


def noise(rng, extent, deviation, most, shards=(), dtype=jnp.bfloat16):
    loudness = steps_of(rng, extent, shards, -0.22, 0.18) if shards else 1.0
    result = jax.random.normal(rng, extent, jnp.float32) * deviation * loudness
    return jnp.minimum(jnp.maximum(result, -most), most).astype(dtype)


def setup_inputs(seed: int = 0, part: int = 0) -> dict:
    key_list = jax.random.split(jax.random.key(seed), 10)
    own_keys = jax.random.split(jax.random.fold_in(key_list[9], part), 10)
    return {
        "queries": draw_queries(jax.random.fold_in(jax.random.fold_in(key_list[9], part), 71), part),
        "vision": noise(own_keys[1], (VISION_TOKENS, VISION_WIDTH), 1.0, 6.0, ((0, 8),)),
        "key_matrix": noise(key_list[2], (VISION_WIDTH, KEY_VALUE_HEADS * HEAD_SIZE), VISION_WIDTH ** -0.5, 0.0625, ((0, 8), (1, 2))),
        "value_matrix": noise(key_list[3], (VISION_WIDTH, KEY_VALUE_HEADS * HEAD_SIZE), VISION_WIDTH ** -0.5, 0.0625, ((0, 8), (1, 2))),
        "out_weight": noise(key_list[4], (QUERY_HEADS * HEAD_SIZE, D), (QUERY_HEADS * HEAD_SIZE) ** -0.5, 0.09375, ((0, 2), (1, 8))),
        "residual": noise(own_keys[5], (TEXT_TOKENS, D), 0.3, 4.0, ((0, 2), (1, 8))),
        "query_norm_gain": draw_query_norm_gain(jax.random.fold_in(key_list[9], 71), part),
        "key_norm_gain": draw_key_norm_gain(jax.random.fold_in(key_list[9], 71), part),
        "attn_gate": jnp.clip(jax.random.uniform(key_list[8], (1,), jnp.float32, 0.5, 2.0), 0.5, 2.0),
    }


epsilon = 1e-05

def apply_norm(value_heads, gain):
    return value_heads * lax.rsqrt(lax.optimization_barrier(jnp.mean(value_heads * value_heads, axis=-1, keepdims=True)) + epsilon) * gain

def reference(queries, vision, key_matrix, value_matrix, out_weight, residual, query_norm_gain, key_norm_gain, attn_gate):
    expanded_keys = jnp.dot(vision, key_matrix, preferred_element_type=jnp.float32)
    expanded_values = jnp.dot(vision, value_matrix, preferred_element_type=jnp.float32)
    key_heads = apply_norm(expanded_keys.reshape(VISION_TOKENS, KEY_VALUE_HEADS, HEAD_SIZE), key_norm_gain).astype(jnp.bfloat16)
    value_heads = expanded_values.reshape(VISION_TOKENS, KEY_VALUE_HEADS, HEAD_SIZE).astype(jnp.bfloat16)
    heads_per_group = QUERY_HEADS // KEY_VALUE_HEADS
    norm_result = apply_norm(queries.astype(jnp.float32).reshape(TEXT_TOKENS, KEY_VALUE_HEADS, heads_per_group, HEAD_SIZE), query_norm_gain).astype(jnp.bfloat16)
    rows_per_block = 128 if TEXT_TOKENS % 128 == 0 else TEXT_TOKENS
    blocked_queries = norm_result.reshape(TEXT_TOKENS // rows_per_block, rows_per_block, KEY_VALUE_HEADS, heads_per_group, HEAD_SIZE)
    keys_wide = key_heads.astype(jnp.float32)
    values_wide = value_heads.astype(jnp.float32)

    def attend_block(query_block):
        scores = jnp.einsum('tgqd,rgd->tgqr', query_block.astype(jnp.float32), keys_wide) * HEAD_SIZE ** (-0.5)
        maxima = lax.optimization_barrier(jnp.max(scores, axis=-1, keepdims=True))
        weights = jnp.exp(scores - maxima)
        denominator = lax.optimization_barrier(jnp.sum(weights, axis=-1))
        rounded = lax.optimization_barrier(weights.astype(jnp.bfloat16))
        numerator = jnp.einsum('tgqr,rgd->tgqd', rounded.astype(jnp.float32), values_wide)
        return (numerator / denominator[..., None]).astype(jnp.bfloat16)
    attended = lax.map(attend_block, blocked_queries).reshape(TEXT_TOKENS, QUERY_HEADS * HEAD_SIZE)
    projected = jnp.dot(attended, out_weight, preferred_element_type=jnp.float32)
    return (residual.astype(jnp.float32) + jnp.tanh(attn_gate[0]) * projected).astype(jnp.bfloat16)
```

```python
import functools

import jax
import jax.numpy as jnp
from jax import lax
from jax.experimental import pallas as pl
from jax.experimental.pallas import tpu as pltpu
from jax.sharding import PartitionSpec as P

HEAD_SIZE = 128
EPSILON = 1e-05
MESH = pl.DeviceIdType.MESH


def ring_columns(mesh):
    line = mesh.devices[0, :, 0]
    coords = [getattr(d, "coords", None) for d in line]
    if any(c is None for c in coords):
        return 1
    n = len(coords)

    def hops(order):
        return sum(
            sum(abs(a - b) for a, b in zip(coords[order[i]], coords[order[(i + 1) % n]]))
            for i in range(n)
        )

    straight = list(range(n))
    folded = straight[0::2] + straight[1::2][::-1]
    return 2 if n % 4 == 0 and hops(folded) < hops(straight) else 1


def line_split(rows, pairs):
    shared = rows * 19 // 40 // 16 * 16 if pairs else 0
    return shared, rows - shared


def norm(x, gain):
    return x * lax.rsqrt(jnp.mean(x * x, axis=-1, keepdims=True) + EPSILON) * gain


def kernel(
    n, folds, pairs,
    q_ref, vision_ref, key_ref, value_ref, out_w_ref, res_ref, qgain_ref, kgain_ref, gate_ref,
    out_ref,
    wk, wv, vis, ow, kbuf, vbuf, a0, a1, qs, pout, pin, kown, kout, kin, vout, vin,
    load_sem, wsend, wrecv, xsend, xrecv, ksend, krecv, asend, arecv, psend, precv,
    ysend, yrecv, csend, crecv,
):
    group = lax.axis_index("groups")
    me = lax.axis_index("seq")
    head = lax.axis_index("head")
    half = n // folds

    def position(i):
        if folds == 1:
            return i
        z, y = i // 2, i % 2
        return z * (1 - y) + (n - 1 - z) * y

    def index(p):
        if folds == 1:
            return p
        y = p // half
        z = p * (1 - y) + (n - 1 - p) * y
        return z * 2 + y

    pos = position(me)

    def at(offset):
        return index(lax.rem(pos + (n + offset), n))

    neighbours = {1: at(1), -1: at(-1)}
    streams = [(1, 0, n // 2), (-1, 1, n // 2), (1, 1, n // 2 - 1), (-1, 0, n // 2 - 1)]

    def piece(view, send, recv, t, s, received):
        direction, b, _ = streams[t]
        owner = at(-direction * (s + received))
        v = view(b, owner)
        return pltpu.make_async_remote_copy(
            src_ref=v, dst_ref=v, send_sem=send.at[t, s], recv_sem=recv.at[t, s],
            device_id={"seq": neighbours[direction]}, device_id_type=MESH,
        )

    def begin(view, send, recv, b):
        for t, stream in enumerate(streams):
            if stream[1] == b and stream[2] > 0:
                piece(view, send, recv, t, 0, 0).start()

    def run(view, send, recv, arrived=None):
        for s in range(n // 2):
            for t, stream in enumerate(streams):
                if s < stream[2]:
                    piece(view, send, recv, t, s, 1).wait_recv()
                    if s + 1 < stream[2]:
                        piece(view, send, recv, t, s + 1, 0).start()
                    if arrived is not None:
                        arrived(t, s)

    def drain(view, send, recv):
        for t, stream in enumerate(streams):
            for s in range(stream[2]):
                piece(view, send, recv, t, s, 0).wait_send()

    rows = key_ref.shape[0]
    vrows, width = vision_ref.shape
    text = q_ref.shape[0]
    kv_local = key_ref.shape[1] // HEAD_SIZE
    heads_local = q_ref.shape[1] // HEAD_SIZE
    per_group = heads_local // kv_local
    odd = group % 2
    partner = group + 1 - 2 * odd
    weights = (wk, wv)
    mine = pl.ds(pl.multiple_of(me * vrows, 16), vrows)
    bufs = (kbuf, vbuf)
    barrier = pltpu.get_barrier_semaphore()

    def greet(**target):
        pl.semaphore_signal(barrier, inc=1, device_id=target, device_id_type=MESH)

    def kv_view(b, owner):
        return bufs[b].at[pl.ds(pl.multiple_of(owner * vrows, 16), vrows)]

    def queries():
        for h in range(heads_local):
            x = q_ref[:, h * HEAD_SIZE:(h + 1) * HEAD_SIZE].astype(jnp.float32)
            qs[h * text:(h + 1) * text, :] = norm(x, qgain_ref[...]).astype(jnp.bfloat16)

    def store_keys(keys):
        for g in range(kv_local):
            cols = slice(g * HEAD_SIZE, (g + 1) * HEAD_SIZE)
            kbuf[mine, cols] = norm(keys[:, cols], kgain_ref[...]).astype(jnp.bfloat16)

    def line_phase():
        nz = half
        z, y = me // 2, me % 2
        other = z * 2 + 1 - y
        padded = wk.shape[0] // nz
        lead = y * (padded - rows)
        shared, ringed = line_split(rows, pairs)
        middle = ringed - shared

        def slot(b, zz, start, size):
            at_row = pl.multiple_of(zz * padded + lead + start, 16)
            return weights[b].at[pl.ds(at_row, size)]

        parts = [(odd * ringed, shared), (shared, middle)] if pairs else [(0, rows)]
        loads = [
            pltpu.make_async_copy(key_ref, slot(0, z, 0, rows), load_sem.at[0]),
            pltpu.make_async_copy(value_ref, slot(1, z, 0, rows), load_sem.at[1]),
            pltpu.make_async_copy(out_w_ref, ow, load_sem.at[3]),
        ]
        for zz in range(nz):
            column = pl.multiple_of(zz * 2 * rows + y * (2 * rows - padded), HEAD_SIZE)
            loads.append(pltpu.make_async_copy(
                vision_ref.at[:, pl.ds(column, padded)],
                vis.at[:vrows, zz * padded:(zz + 1) * padded], load_sem.at[4 + zz],
            ))
        loads[0].start()
        loads[1].start()
        greet(seq=other)
        greet(head=1 - head)
        if pairs:
            greet(groups=partner)

        @pl.when(z > 0)
        def _():
            greet(seq=(z - 1) * 2 + y)

        @pl.when(z < nz - 1)
        def _():
            greet(seq=(z + 1) * 2 + y)

        if padded > rows:
            for zz in range(nz):
                for w in weights:
                    start = pl.multiple_of(zz * padded + (1 - y) * rows, 16)
                    w[pl.ds(start, padded - rows), :] = jnp.zeros(
                        (padded - rows, w.shape[1]), w.dtype)

        peers = (3 if pairs else 2) + (z + nz - 1) // nz + (2 * nz - 2 - z) // nz
        pl.semaphore_wait(barrier, peers)

        def hop(b, d, s, part, zz):
            start, size = parts[part]
            v = slot(b, zz, start, size)
            k = (b * 2 + (d + 1) // 2) * 2 + part
            return pltpu.make_async_remote_copy(
                src_ref=v, dst_ref=v, send_sem=wsend.at[k, s], recv_sem=wrecv.at[k, s],
                device_id={"seq": (z + d) * 2 + y}, device_id_type=MESH,
            )

        def cross(b, d, s, zz, received):
            which = (1 - odd) if received else odd
            v = slot(b, zz, which * ringed, shared)
            k = b * 2 + (d + 1) // 2
            return pltpu.make_async_remote_copy(
                src_ref=v, dst_ref=v, send_sem=xsend.at[k, s], recv_sem=xrecv.at[k, s],
                device_id={"groups": partner}, device_id_type=MESH,
            )

        def can_send(d, s):
            ahead = (z < nz - 1) if d == 1 else (z > 0)
            behind = (z >= s) if d == 1 else (z + s <= nz - 1)
            return jnp.logical_and(ahead, behind)

        def gets(d, s):
            return (z > s) if d == 1 else (z + s < nz - 1)

        half_rows = vrows // 2

        def vision_out(zz):
            r = pl.ds(pl.multiple_of(head * half_rows, 16), half_rows)
            column = pl.multiple_of(zz * 2 * rows + (1 - y) * (2 * rows - padded), HEAD_SIZE)
            to = pl.ds(pl.multiple_of(vrows + head * half_rows, 16), half_rows)
            return pltpu.make_async_remote_copy(
                src_ref=vision_ref.at[r, pl.ds(column, padded)],
                dst_ref=vis.at[to, zz * padded:(zz + 1) * padded],
                send_sem=ysend.at[zz], recv_sem=yrecv.at[zz],
                device_id={"seq": other}, device_id_type=MESH,
            )

        def vision_pass(zz, received):
            which = (1 - head) if received else head
            r = pl.ds(pl.multiple_of(vrows + which * half_rows, 16), half_rows)
            v = vis.at[r, zz * padded:(zz + 1) * padded]
            return pltpu.make_async_remote_copy(
                src_ref=v, dst_ref=v, send_sem=csend.at[zz], recv_sem=crecv.at[zz],
                device_id={"head": 1 - head}, device_id_type=MESH,
            )

        def begin_line(b):
            loads[b].wait()
            for d in (1, -1):
                @pl.when(can_send(d, 0))
                def _():
                    for part in range(len(parts)):
                        hop(b, d, 0, part, z).start()

        def step(b, s):
            for part in range(len(parts)):
                for d in (1, -1):
                    zz = z - d * (s + 1)

                    @pl.when(gets(d, s))
                    def _():
                        hop(b, d, s, part, zz).wait_recv()
                        if s + 1 < nz - 1:
                            @pl.when(can_send(d, s + 1))
                            def _():
                                hop(b, d, s + 1, part, zz).start()
                        if part == 0 and pairs:
                            cross(b, d, s, zz, False).start()

        def finish(b):
            if pairs:
                for s in range(nz - 1):
                    for d in (1, -1):
                        @pl.when(gets(d, s))
                        def _():
                            cross(b, d, s, z - d * (s + 1), True).wait_recv()

        def give(b):
            src, dst = ((kout, kin), (vout, vin))[b]
            return pltpu.make_async_remote_copy(
                src_ref=src, dst_ref=dst, send_sem=ysend.at[nz + b], recv_sem=yrecv.at[nz + b],
                device_id={"seq": other}, device_id_type=MESH,
            )

        def product(b, first):
            r = slice(0, vrows) if first else slice(vrows, 2 * vrows)
            return jnp.dot(vis[r, :], weights[b][...], preferred_element_type=jnp.float32)

        begin_line(0)
        for zz in range(nz):
            vision_out(zz).start()
        for load in loads[2:]:
            load.start()
        queries()
        for s in range(nz - 1):
            step(0, s)
        begin_line(1)
        finish(0)
        for s in range(nz - 1):
            if s == nz - 2:
                for load in loads[3:]:
                    load.wait()
                for zz in range(nz):
                    vision_out(zz).wait_recv()
                    vision_pass(zz, False).start()
                for zz in range(nz):
                    vision_pass(zz, True).wait_recv()
                kout[...] = product(0, False)
                give(0).start()
                kown[...] = product(0, True)
            step(1, s)
        give(0).wait_recv()
        store_keys(kown[...] + kin[...])
        begin(kv_view, ksend, krecv, 0)
        finish(1)
        vout[...] = product(1, False).astype(vout.dtype)
        give(1).start()
        values = product(1, True)
        give(1).wait_recv()
        vbuf[mine, :] = (values + vin[...].astype(jnp.float32)).astype(jnp.bfloat16)
        begin(kv_view, ksend, krecv, 1)

        def settle():
            for b in range(2):
                give(b).wait_send()
                for s in range(nz - 1):
                    for d in (1, -1):
                        @pl.when(can_send(d, s))
                        def _():
                            for part in range(len(parts)):
                                hop(b, d, s, part, z - d * s).wait_send()

                        if pairs:
                            @pl.when(gets(d, s))
                            def _():
                                cross(b, d, s, z - d * (s + 1), False).wait_send()
            for zz in range(nz):
                vision_out(zz).wait_send()
                vision_pass(zz, False).wait_send()

        return loads[2], settle

    def ring_phase():
        own = pl.ds(pl.multiple_of(me * rows, 16), rows)
        loads = [
            pltpu.make_async_copy(key_ref, wk.at[own], load_sem.at[0]),
            pltpu.make_async_copy(value_ref, wv.at[own], load_sem.at[1]),
            pltpu.make_async_copy(vision_ref, vis, load_sem.at[2]),
            pltpu.make_async_copy(out_w_ref, ow, load_sem.at[3]),
        ]
        for load in loads:
            load.start()
        for target in neighbours.values():
            greet(seq=target)
        greet(head=1 - head)
        if pairs:
            greet(groups=partner)
        pl.semaphore_wait(barrier, 4 if pairs else 3)
        loads[0].wait()
        loads[1].wait()
        shared = (rows * 3 // 10 + 15) // 16 * 16 if pairs else 0
        ringed = rows - shared

        def weight_view(b, owner):
            start = owner * rows
            if pairs:
                start = start + odd * shared
            return weights[b].at[pl.ds(pl.multiple_of(start, 16), ringed)]

        def cross(t, s, received):
            direction, b, _ = streams[t]
            owner = at(-direction * (s + 1))
            which = (1 - odd) if received else odd
            start = owner * rows + which * ringed
            v = weights[b].at[pl.ds(pl.multiple_of(start, 16), shared)]
            return pltpu.make_async_remote_copy(
                src_ref=v, dst_ref=v, send_sem=xsend.at[t, s], recv_sem=xrecv.at[t, s],
                device_id={"groups": partner}, device_id_type=MESH,
            )

        begin(weight_view, wsend, wrecv, 0)
        begin(weight_view, wsend, wrecv, 1)
        queries()
        run(weight_view, wsend, wrecv,
            (lambda t, s: cross(t, s, False).start()) if pairs else None)
        if pairs:
            for t, stream in enumerate(streams):
                for s in range(stream[2]):
                    cross(t, s, True).wait_recv()
        loads[2].wait()
        store_keys(jnp.dot(vis[...], wk[...], preferred_element_type=jnp.float32))
        begin(kv_view, ksend, krecv, 0)
        values = jnp.dot(vis[...], wv[...], preferred_element_type=jnp.float32)
        vbuf[mine, :] = values.astype(jnp.bfloat16)
        begin(kv_view, ksend, krecv, 1)

        def settle():
            drain(weight_view, wsend, wrecv)
            if pairs:
                for t, stream in enumerate(streams):
                    for s in range(stream[2]):
                        cross(t, s, False).wait_send()

        return loads[3], settle

    out_load, settle = (line_phase if folds == 2 else ring_phase)()
    run(kv_view, ksend, krecv)

    total = kbuf.shape[0]
    block = min(total, 2048)
    scale = HEAD_SIZE ** (-0.5)
    attended = (a0, a1)
    mine_text = pl.ds(pl.multiple_of(me * text, 16), text)

    def text_view(b, owner):
        return attended[b].at[pl.ds(pl.multiple_of(owner * text, 16), text)]

    groups_per_buffer = kv_local // 2
    for g in range(kv_local):
        cols = slice(g * HEAD_SIZE, (g + 1) * HEAD_SIZE)
        q = qs[g * per_group * text:(g + 1) * per_group * text, :]
        top = None
        for r in range(0, total, block):
            scores = lax.dot_general(
                q, kbuf[r:r + block, cols], (((1,), (1,)), ((), ())),
                preferred_element_type=jnp.float32,
            ) * scale
            high = jnp.max(scores, axis=-1, keepdims=True)
            new = high if top is None else jnp.maximum(top, high)
            weight = jnp.exp(scores - new)
            part = jnp.sum(weight, axis=-1, keepdims=True)
            product = jnp.dot(
                weight.astype(jnp.bfloat16), vbuf[r:r + block, cols],
                preferred_element_type=jnp.float32,
            )
            if top is None:
                den, num = part, product
            else:
                rescale = jnp.exp(top - new)
                den, num = den * rescale + part, num * rescale + product
            top = new
        result = (num / den).astype(jnp.bfloat16)
        b, inner = g // groups_per_buffer, g % groups_per_buffer
        for h in range(per_group):
            column = (inner * per_group + h) * HEAD_SIZE
            attended[b][mine_text, column:column + HEAD_SIZE] = result[h * text:(h + 1) * text, :]
        if inner == groups_per_buffer - 1:
            begin(text_view, asend, arecv, b)
    run(text_view, asend, arecv)
    out_load.wait()

    out_rows = out_ref.shape[0]
    depth = a0.shape[1]

    def project(which):
        r = pl.ds(pl.multiple_of(which * out_rows, 16), out_rows)
        return jnp.dot(
            a0[r, :], ow[:depth, :], preferred_element_type=jnp.float32
        ) + jnp.dot(a1[r, :], ow[depth:, :], preferred_element_type=jnp.float32)

    pout[...] = project(1 - head).astype(jnp.bfloat16)
    swap = pltpu.make_async_remote_copy(
        src_ref=pout, dst_ref=pin, send_sem=psend, recv_sem=precv,
        device_id={"head": 1 - head}, device_id_type=MESH,
    )
    swap.start()
    projected = project(head)
    swap.wait_recv()
    out_ref[...] = (
        res_ref[...].astype(jnp.float32)
        + jnp.tanh(gate_ref[...]) * (projected + pin[...].astype(jnp.float32))
    ).astype(out_ref.dtype)

    swap.wait_send()
    settle()
    drain(kv_view, ksend, krecv)
    drain(text_view, asend, arecv)


def line_kernel(
    n, cuts, extra, offload,
    q_arg, vision_ref, key_ref, value_ref, out_w_ref, res_arg, qgain_arg, kgain_arg, gate_arg,
    out_ref,
    wk, wv, vis, visx, ow, qout, qall, kacc, vacc, kswap, kswap16, vswap, finals, probs, stats, stat_in,
    own_num, rs_out, rs_in, att, total, pout, pin, q_ref, res_ref, qgain_ref, kgain_ref, gate_ref,
    load_sem, send_sem, recv_sem,
):
    group = lax.axis_index("groups")
    me = lax.axis_index("seq")
    head = lax.axis_index("head")
    z, y = me // 2, me % 2
    odd = group % 2
    side = z // 2
    outer = jnp.logical_or(z == 0, z == 3)
    inner = jnp.logical_not(outer)
    pos = {"e": 3 * side, "m": 1 + side, "M": 2 - side, "E": 3 - 3 * side}
    peers = {
        "x": {"groups": group + 1 - 2 * odd}, "y": {"seq": z * 2 + 1 - y}, "h": {"head": 1 - head},
        "e": {"seq": pos["e"] * 2 + y}, "m": {"seq": pos["m"] * 2 + y}, "M": {"seq": pos["M"] * 2 + y},
    }
    rows, cols = key_ref.shape
    vrows = vision_ref.shape[0]
    text = q_arg.shape[0]
    seen = 2 * vrows
    half_rows = vrows // 2
    padded = wk.shape[0] // 4
    lead = y * (padded - rows)
    chunk = rows // cuts
    split = cuts // 2
    per_group = qall.shape[0]
    tokens = n * text // 2
    wide = per_group * HEAD_SIZE
    bf16, f32 = jnp.bfloat16, jnp.float32
    pieces = 8
    width = wide // pieces
    middle = pieces // 2
    group_heads = per_group // pieces
    weights, sources = (wk, wv), (key_ref, value_ref)
    accs, swaps = (kacc, vacc), (kswap, vswap)
    ids = {"to": {}, "from": {}}
    single = {
        "to": ({"out", "qe", "vx", "up"}, {"mid", "in", "fwd", "qm", "vp", "st", "rs", "ax", "ae", "far"}),
        "from": ({"in", "ae"}, {"out", "mid", "fwd", "qe", "qm", "vx", "vp", "up", "st", "rs", "ax", "far"}),
    }

    def near(rel):
        return "n" if rel in ("e", "m") else rel

    def group_of(way, key):
        kind = key[0]
        if kind == "x":
            return "x", key[1], near(key[2])
        if kind == "s":
            return ("far",) if key[2] else ("s", key[1])
        if kind == "vp":
            return ("vp",)
        if way == "from":
            return ("ay", key[1], key[1] * (key[2] // middle)) if kind == "ay" else key
        if kind in ("out", "mid", "fwd"):
            return key[:2]
        if kind == "in":
            return key[:3]
        return (kind,) if kind in ("yv", "yp", "vx", "rs", "ax", "ae", "ay") else key

    def ident(way, group):
        both, roles = ids[way], single[way]
        role = 1 if group[0] in roles[0] else 2 if group[0] in roles[1] else 0
        if group not in both:
            both[group] = role, sum(1 for r, _ in both.values() if r == role)
        role, i = both[group]
        return i if role == 0 else shared[way] + i

    def copy(key, src, dst, to):
        out, into = (ident(way, group_of(way, key)) for way in ("to", "from"))
        return pltpu.make_async_remote_copy(
            src_ref=src, dst_ref=dst, send_sem=send_sem.at[out], recv_sem=recv_sem.at[into],
            device_id=peers[to], device_id_type=MESH,
        )

    def got(key, dst):
        copy(key, dst, dst, "h").wait_recv()

    def sender(log):
        def send(key, view, to):
            src, dst = view() if callable(view) else view
            copy(key, src, dst, to).start()
            log.setdefault(group_of("to", key), []).append(key)
        return send

    def bulk(group, count):
        kind = group[0]
        if kind in ("x", "out", "mid", "in", "fwd"):
            return weights[group[1]].at[pl.ds(0, count * chunk)]
        if kind in ("yv", "yp"):
            return vis.at[pl.ds(0, count * half_rows), pl.ds(0, padded)]
        if kind in ("vx", "vp"):
            return visx.at[pl.ds(0, count * half_rows)]
        if kind in ("s", "far"):
            return swaps[group[1] if kind == "s" else 1].at[0, 0]
        if kind == "up":
            return kswap16.at[0] if group[1] == 0 else vswap.at[2, 0]
        if kind in ("qe", "qm"):
            return qall.at[:, pl.ds(0, 2 * text if kind == "qe" else tokens)]
        if kind == "ax":
            return att.at[0, pl.ds(0, tokens)]
        return {"q": qout, "st": stat_in, "rs": rs_out, "ae": att.at[0], "ay": att.at[0], "p": pout}[kind]

    def drain(log):
        for group, keys in log.items():
            view = bulk(group, len(keys))
            copy(keys[0], view, view, "h").wait_send()

    shared = {"to": 13, "from": 21}
    outer_log, inner_log, log = {}, {}, {}

    def start_of(j, which):
        return j * chunk + which * (rows - chunk - 2 * chunk * j)

    def slot(b, rel, start, size=chunk):
        return weights[b].at[pl.ds(pl.multiple_of(pos[rel] * padded + lead + start, 16), size)]

    def mine(b, rel, j):
        return slot(b, rel, start_of(j, odd))

    def theirs(b, rel, j):
        return slot(b, rel, start_of(j, 1 - odd))

    def source(b, j):
        return sources[b].at[pl.ds(pl.multiple_of(start_of(j, odd), 16), chunk)]

    def column(yy, zz):
        return pl.ds(pl.multiple_of(zz * 2 * rows + yy * (2 * rows - padded), HEAD_SIZE), padded)

    def block(rel):
        return pl.ds(pl.multiple_of(pos[rel] * padded, HEAD_SIZE), padded)

    def part(which, far):
        return pl.ds(pl.multiple_of(far * vrows + which * half_rows, 16), half_rows)

    def lanes(which):
        return pl.ds(pl.multiple_of(which * HEAD_SIZE, HEAD_SIZE), HEAD_SIZE)

    def piece(c):
        return slice(c * width, (c + 1) * width)

    def span(which):
        return pl.ds(pl.multiple_of(which * tokens, 16), tokens)

    def crossed(b, rel, count):
        got(("x", b, rel, 0), slot(b, rel, 0, count * chunk))

    def vision_send(send, i, rel):
        send(("yv", i), lambda: (vision_ref.at[part(head, 0), column(1 - y, pos[rel])],
                                 vis.at[part(head, 1), block(rel)]), "y")

    def vision_pass(send, i, rel):
        got(("yv", i), vis.at[part(head, 1), block(rel)])
        send(("yp", i), lambda: (vis.at[part(head, 1), block(rel)],) * 2, "h")

    def vision_done(i, rel):
        got(("yp", i), vis.at[part(1 - head, 1), block(rel)])

    def give(send, b, x):
        swap = swaps[b]
        swap[x, 0] = accs[b][x, :, lanes(1 - y)].astype(swap.dtype)
        for k in range(2):
            send(("s", b, x, k), lambda k=k: (swap.at[x, 0, pl.ds(k * vrows, vrows)],
                                              swap.at[x, 1, pl.ds((1 - k) * vrows, vrows)]), "y")

    def take(b, x):
        got(("s", b, x, 0), swaps[b].at[x, 1])
        return accs[b][x, :, lanes(y)] + swaps[b][x, 1].astype(f32)

    def multiply(b, rel, start):
        part = jnp.dot(vis[:, block(rel)], weights[b][block(rel), :], preferred_element_type=f32)
        accs[b][0] = part if start else accs[b][0] + part

    loads = [
        pltpu.make_async_copy(sources[b], weights[b].at[pl.ds(pl.multiple_of(z * padded + lead, 16), rows)], load_sem.at[b])
        for b in range(2)
    ]
    for zz in range(4):
        loads.append(pltpu.make_async_copy(
            vision_ref.at[:, column(y, zz)], vis.at[:vrows, zz * padded:(zz + 1) * padded],
            load_sem.at[2 + zz]))
    out_load = pltpu.make_async_copy(out_w_ref, ow, load_sem.at[6])
    small = [
        pltpu.make_async_copy(src, dst, load_sem.at[7 + i])
        for i, (src, dst) in enumerate([
            (q_arg, q_ref), (qgain_arg, qgain_ref), (kgain_arg, kgain_ref), (gate_arg, gate_ref), (res_arg, res_ref)])
    ]
    for load in small:
        load.start()

    barrier = pltpu.get_barrier_semaphore()

    def greet(to):
        pl.semaphore_signal(barrier, inc=1, device_id=peers[to], device_id_type=MESH)

    greet("y")
    greet("h")
    greet("x")

    @pl.when(outer)
    def _():
        greet("m")
        pl.semaphore_wait(barrier, 4)

    @pl.when(inner)
    def _():
        greet("e")
        greet("M")
        pl.semaphore_wait(barrier, 5)

    first = split + extra
    order_e = ("E", "e", "m", "M")
    order_m = ("m", "e", "M", "E")
    inward = (("m", "M", "E"), ("m", "M") if offload else ("m", "M", "E"))

    @pl.when(outer)
    def _():
        send = sender(outer_log)
        for j in range(first):
            send(("out", 0, j), lambda j=j: (source(0, j), mine(0, "e", j)), "m")
        vision_send(send, 0, order_e[0])

    @pl.when(inner)
    def _():
        send = sender(inner_log)
        for j in range(split):
            send(("mid", 0, j), lambda j=j: (source(0, j), mine(0, "m", j)), "M")
            send(("in", 0, "m", j), lambda j=j: (source(0, j), mine(0, "m", j)), "e")
        vision_send(send, 0, order_m[0])

    for load in loads:
        load.start()
    out_load.start()
    for w in weights:
        for zz in range(4):
            at = pl.multiple_of(zz * padded + (1 - y) * rows, 16)
            w[pl.ds(at, padded - rows), :] = jnp.zeros((padded - rows, cols), w.dtype)

    for load in small:
        load.wait()
    own_tokens = pl.ds(pl.multiple_of(me * text, 16), text)
    far_tokens = pl.ds(pl.multiple_of((z * 2 + 1 - y) * text, 16), text)
    for h in range(per_group):
        for which in (1 - y, y):
            at = pl.ds(pl.multiple_of(which * wide + h * HEAD_SIZE, HEAD_SIZE), HEAD_SIZE)
            value = norm(q_ref[:, at].astype(f32), qgain_ref[...]).astype(bf16)
            if which is y:
                qall[h, own_tokens, :] = value
            else:
                qout[h] = value
    sender(log)(("q",), lambda: (qout, qall.at[:, own_tokens, :]), "y")

    def line_tokens(zz):
        return qall.at[:, pl.ds(pl.multiple_of(zz * 2 * text, 16), 2 * text), :]

    def side_tokens(which):
        return qall.at[:, span(which), :]

    @pl.when(outer)
    def _():
        send = sender(outer_log)
        for i in range(1, 4):
            vision_send(send, i, order_e[i])

        def inbound(b, rel):
            for j in range(split):
                got(("in", b, rel, j), mine(b, rel, j))
                send(("x", b, rel, j), lambda b=b, rel=rel, j=j: (mine(b, rel, j),) * 2, "x")

        for j in range(first):
            send(("out", 1, j), lambda j=j: (source(1, j), mine(1, "e", j)), "m")
        inbound(0, "m")
        got(("q",), qall.at[:, far_tokens, :])
        send(("qe",), lambda: (line_tokens(z), line_tokens(z)), "m")
        if offload:
            send(("vx", 0), lambda: (vision_ref.at[part(head, 0), column(y, pos["E"])],
                                     visx.at[part(head, 0)]), "m")
        vision_pass(send, 0, "E")
        if offload:
            send(("vx", 1), lambda: (vis.at[part(head, 1), block("E")], visx.at[part(head, 1)]), "m")
        inbound(0, "M")
        vision_pass(send, 1, "e")
        inbound(0, "E")
        vision_pass(send, 2, "m")
        inbound(1, "m")
        for load in loads:
            load.wait()
        for i, rel in enumerate(order_e[:3]):
            vision_done(i, rel)
            if rel != "e":
                crossed(0, rel, split)
            multiply(0, rel, i == 0)
        vision_pass(send, 3, "M")
        crossed(0, "M", split)
        vision_done(3, "M")
        multiply(0, "M", False)
        give(send, 0, 0)
        multiply(1, "e", True)
        crossed(1, "m", split)
        multiply(1, "m", False)
        for rel in inward[1][1:]:
            inbound(1, rel)
        for rel in inward[1][1:]:
            crossed(1, rel, split)
            multiply(1, rel, False)
        give(send, 1, 0)
        kswap16[0] = norm(take(0, 0), kgain_ref[...]).astype(bf16)
        send(("up", 0), lambda: (kswap16.at[0], kswap16.at[1]), "m")
        vswap[2, 0] = take(1, 0).astype(bf16)
        send(("up", 1), lambda: (vswap.at[2, 0], vswap.at[2, 1]), "m")

    @pl.when(inner)
    def _():
        send = sender(inner_log)
        for i in range(1, 4):
            vision_send(send, i, order_m[i])


        def from_end(b, j):
            got(("out", b, j), mine(b, "e", j))
            if j < split:
                send(("fwd", b, j), lambda: (mine(b, "e", j),) * 2, "M")
            if j < cuts - first:
                send(("x", b, "e", j), lambda: (mine(b, "e", j),) * 2, "x")

        def from_middle(b, j):
            got(("mid", b, j), mine(b, "M", j))
            send(("in", b, "M", j), lambda: (mine(b, "M", j),) * 2, "e")
            send(("x", b, "M", j), lambda: (mine(b, "M", j),) * 2, "x")

        def from_far_end(b, j):
            got(("fwd", b, j), mine(b, "E", j))
            if "E" in inward[b]:
                send(("in", b, "E", j), lambda: (mine(b, "E", j),) * 2, "e")
            send(("x", b, "E", j), lambda: (mine(b, "E", j),) * 2, "x")

        for j in range(first):
            from_end(0, j)
            if j < split:
                from_middle(0, j)
        for j in range(split):
            send(("mid", 1, j), lambda j=j: (source(1, j), mine(1, "m", j)), "M")
        for j in range(split):
            from_far_end(0, j)
        for j in range(split):
            send(("in", 1, "m", j), lambda j=j: (source(1, j), mine(1, "m", j)), "e")
        vision_pass(send, 0, "m")
        for j in range(first):
            from_end(1, j)
        got(("q",), qall.at[:, far_tokens, :])
        vision_pass(send, 1, "e")
        for j in range(split):
            from_middle(1, j)
        got(("qe",), line_tokens(pos["e"]))
        send(("qm",), lambda: (side_tokens(side),) * 2, "M")
        vision_pass(send, 2, "M")
        for j in range(split):
            from_far_end(1, j)
        for load in loads:
            load.wait()
        crossings = {"m": 0, "e": cuts - first, "M": split, "E": split}
        for i, rel in enumerate(order_m[:3]):
            vision_done(i, rel)
            crossed(0, rel, crossings[rel])
            multiply(0, rel, i == 0)
        vision_pass(send, 3, "E")
        crossed(0, "E", split)
        vision_done(3, "E")
        multiply(0, "E", False)
        give(send, 0, 0)
        multiply(1, "m", True)
        crossed(1, "e", cuts - first)
        multiply(1, "e", False)
        if offload:
            for k in range(2):
                got(("vx", k), visx.at[part(head, k)])
                send(("vp", k), lambda k=k: (visx.at[part(head, k)],) * 2, "h")
        crossed(1, "M", split)
        multiply(1, "M", False)
        crossed(1, "E", split)
        multiply(1, "E", False)
        give(send, 1, 0)
        if offload:
            got(("vp", 0), visx.at[pl.ds(0, vrows)])
            vacc[1] = jnp.dot(visx[...], wv[block("E"), :], preferred_element_type=f32)
            give(send, 1, 1)
        got(("qm",), side_tokens(1 - side))

        lane = lax.broadcasted_iota(jnp.int32, (2 * tokens, HEAD_SIZE), 1)
        scale = HEAD_SIZE ** (-0.5)

        def score(r):
            k = finals[0, r * seen:(r + 1) * seen, :]
            tops = jnp.zeros((2 * tokens, HEAD_SIZE), f32)
            dens = jnp.ones((2 * tokens, HEAD_SIZE), f32)
            for h in range(per_group):
                s = lax.dot_general(
                    qall[h], k, (((1,), (1,)), ((), ())), preferred_element_type=f32) * scale
                top = jnp.max(s, axis=-1, keepdims=True)
                p = jnp.exp(s - top)
                den = jnp.sum(p, axis=-1, keepdims=True)
                probs[h, :, r * seen:(r + 1) * seen] = p.astype(bf16)
                tops = jnp.where(lane == h, top, tops)
                dens = jnp.where(lane == h, den, dens)
            stats[r, 0] = tops
            stats[r, 1] = dens

        finals[0, :seen, :] = norm(take(0, 0), kgain_ref[...]).astype(bf16)
        score(0)
        got(("up", 0), kswap16.at[1])
        finals[0, seen:, :] = kswap16[1]
        score(1)

        def merge(top_a, den_a, top_b, den_b):
            top = jnp.maximum(top_a, top_b)
            fa, fb = jnp.exp(top_a - top), jnp.exp(top_b - top)
            return top, fa * den_a + fb * den_b, fa, fb

        top, den, f0, f1 = merge(stats[0, 0], stats[0, 1], stats[1, 0], stats[1, 1])
        stats[0, 0] = f0
        stats[1, 0] = f1
        stats[2, 0] = top
        stats[2, 1] = den
        send(("st",), lambda: (stats.at[2, :, span(1 - side)], stat_in), "M")

        finals[1, :seen, :] = take(1, 0).astype(bf16)
        far_values = take(1, 1) if offload else 0.0
        got(("up", 1), vswap.at[2, 1])
        finals[1, seen:, :] = (far_values + vswap[2, 1].astype(f32)).astype(bf16)
        got(("st",), stat_in)
        _, den, fs, fo = merge(stats[2, 0, span(side), :], stats[2, 1, span(side), :], stat_in[0], stat_in[1])
        inverse = 1.0 / den
        other = fo * inverse
        mine0 = fs * inverse * stats[0, 0, span(side), :]
        mine1 = fs * inverse * stats[1, 0, span(side), :]
        far0, far1 = stats[0, 0, span(1 - side), :], stats[1, 0, span(1 - side), :]

        def numerator(h, which, c0, c1):
            p = probs[h, span(which), :]
            return (c0[:, h:h + 1] * jnp.dot(p[:, :seen], finals[1, :seen, :], preferred_element_type=f32)
                    + c1[:, h:h + 1] * jnp.dot(p[:, seen:], finals[1, seen:, :], preferred_element_type=f32))


        for c in range(pieces):
            for h in range(c * group_heads, (c + 1) * group_heads):
                rs_out[:, h * HEAD_SIZE:(h + 1) * HEAD_SIZE] = numerator(h, 1 - side, far0, far1).astype(bf16)
            send(("rs", c), lambda c=c: (rs_out.at[:, piece(c)], rs_in.at[:, piece(c)]), "M")
        for h in range(per_group):
            own_num[:, h * HEAD_SIZE:(h + 1) * HEAD_SIZE] = numerator(h, side, mine0, mine1)
        for c in range(pieces):
            got(("rs", c), rs_in.at[:, piece(c)])
            for h in range(c * group_heads, (c + 1) * group_heads):
                at = slice(h * HEAD_SIZE, (h + 1) * HEAD_SIZE)
                att[y, span(side), at] = (
                    own_num[:, at] + other[:, h:h + 1] * rs_in[:, at].astype(f32)).astype(bf16)
            here = lambda c=c: (att.at[y, span(side), piece(c)],) * 2
            send(("ax", c), here, "M")
            send(("ae", 0, c), here, "e")
            send(("ay", 0, c), here, "y")

    out_load.wait()

    def forward(t, c):
        view = lambda: (att.at[y, span(side if t == 0 else 1 - side), piece(c)],) * 2

        @pl.when(outer)
        def _():
            got(("ae", t, c), view()[0])
            sender(outer_log)(("ay", t, c), view, "y")

        if t == 1:
            @pl.when(inner)
            def _():
                send = sender(inner_log)
                got(("ax", c), view()[0])
                send(("ae", 1, c), view, "e")
                send(("ay", 1, c), view, "y")

    def project(t, which, start, stop):
        if which is not y:
            got(("ay", t, start), att.at[
                which, span(side if t == 0 else 1 - side), start * width:stop * width])
        depth = (stop - start) * width
        part = jnp.dot(
            att[which, span(side if t == 0 else 1 - side), start * width:stop * width],
            ow[pl.ds(pl.multiple_of(which * wide + start * width, 16), depth), :],
            preferred_element_type=f32)
        total[t] = part if which is y and start == 0 else total[t] + part

    def settle(t):
        which = side if t == 0 else 1 - side

        @pl.when(which != head)
        def _():
            pout[...] = total[t].astype(bf16)
            copy(("p",), pout, pin, "h").start()

    other = 1 - y
    for c in range(pieces):
        forward(0, c)
    project(0, y, 0, pieces)
    for c in range(middle):
        forward(1, c)
    project(0, other, 0, pieces)
    settle(0)
    for c in range(middle, pieces):
        forward(1, c)
    project(1, y, 0, pieces)
    project(1, other, 0, middle)
    project(1, other, middle, pieces)
    settle(1)
    mine_first = side == head
    projected = jnp.where(mine_first, total[0], total[1])
    got(("p",), pin)
    out_ref[...] = (
        res_ref[...].astype(f32)
        + jnp.tanh(gate_ref[...]) * (projected + pin[...].astype(f32))
    ).astype(out_ref.dtype)
    log["p",] = [("p",)]

    @pl.when(outer)
    def _():
        drain(outer_log)

    @pl.when(inner)
    def _():
        drain(inner_log)

    drain(log)
    for way, sem in (("to", send_sem), ("from", recv_sem)):
        counts = [sum(1 for r, _ in ids[way].values() if r == role) for role in range(3)]
        assert counts[0] == shared[way] and sem.shape[0] == counts[0] + max(counts[1:]), (way, counts, sem.shape)


def line_call(n, queries, vision, key_matrix, value_matrix, out_weight, residual):
    rows, columns = key_matrix.shape
    vrows = vision.shape[0]
    text, qcols = queries.shape
    bf16, f32 = jnp.bfloat16, jnp.float32
    padded = -(-rows // HEAD_SIZE) * HEAD_SIZE
    per_group = qcols // HEAD_SIZE // 2
    tokens = n * text // 2
    seen = 2 * vrows
    scratch = [
        pltpu.VMEM((4 * padded, columns), bf16),
        pltpu.VMEM((4 * padded, columns), bf16),
        pltpu.VMEM((seen, 4 * padded), bf16),
        pltpu.VMEM((seen, padded), bf16),
        pltpu.VMEM(out_weight.shape, bf16),
        pltpu.VMEM((per_group, text, HEAD_SIZE), bf16),
        pltpu.VMEM((per_group, 2 * tokens, HEAD_SIZE), bf16),
        pltpu.VMEM((1, seen, columns), f32),
        pltpu.VMEM((2, seen, columns), f32),
        pltpu.VMEM((1, 2, seen, HEAD_SIZE), f32),
        pltpu.VMEM((2, seen, HEAD_SIZE), bf16),
        pltpu.VMEM((3, 2, seen, HEAD_SIZE), bf16),
        pltpu.VMEM((2, 2 * seen, HEAD_SIZE), bf16),
        pltpu.VMEM((per_group, 2 * tokens, 2 * seen), bf16),
        pltpu.VMEM((3, 2, 2 * tokens, HEAD_SIZE), f32),
        pltpu.VMEM((2, tokens, HEAD_SIZE), f32),
        pltpu.VMEM((tokens, qcols // 2), f32),
        pltpu.VMEM((tokens, qcols // 2), bf16),
        pltpu.VMEM((tokens, qcols // 2), bf16),
        pltpu.VMEM((2, 2 * tokens, qcols // 2), bf16),
        pltpu.VMEM((2,) + residual.shape, f32),
        pltpu.VMEM(residual.shape, bf16),
        pltpu.VMEM(residual.shape, bf16),
        pltpu.VMEM(queries.shape, bf16),
        pltpu.VMEM(residual.shape, bf16),
        pltpu.VMEM((1, HEAD_SIZE), f32),
        pltpu.VMEM((1, HEAD_SIZE), f32),
        pltpu.VMEM((1, 1), f32),
        pltpu.SemaphoreType.DMA((12,)),
        pltpu.SemaphoreType.DMA((29,)),
        pltpu.SemaphoreType.DMA((66,)),
    ]
    return functools.partial(line_kernel, n, 6, 1, True), scratch


def body(n, folds, pairs, queries, vision, key_matrix, value_matrix, out_weight, residual,
         query_norm_gain, key_norm_gain, attn_gate):
    rows, columns = key_matrix.shape
    vrows, width = vision.shape
    text, qcols = queries.shape
    bf16 = jnp.bfloat16
    vmem = pl.BlockSpec(memory_space=pltpu.VMEM)
    hbm = pl.BlockSpec(memory_space=pl.ANY)
    steps = pltpu.SemaphoreType.DMA((4, n // 2))
    hops = pltpu.SemaphoreType.DMA((8, n // 2))
    if folds == 2:
        depth = n // 2 * (-(-rows // HEAD_SIZE) * HEAD_SIZE)
        seen = (2 * vrows, depth)
        part = (vrows, columns)
    else:
        depth = n * rows
        seen = (vrows, width)
        part = (16, HEAD_SIZE)
    middle = (
        folds == 2 and n == 8 and pairs and columns == 2 * HEAD_SIZE
        and rows % 96 == 0 and qcols % (8 * HEAD_SIZE) == 0
    )
    if middle:
        run, scratch = line_call(n, queries, vision, key_matrix, value_matrix, out_weight, residual)
    else:
        run, scratch = functools.partial(kernel, n, folds, pairs), [
            pltpu.VMEM((depth, columns), bf16),
            pltpu.VMEM((depth, columns), bf16),
            pltpu.VMEM(seen, bf16),
            pltpu.VMEM(out_weight.shape, bf16),
            pltpu.VMEM((n * vrows, columns), bf16),
            pltpu.VMEM((n * vrows, columns), bf16),
            pltpu.VMEM((n * text, qcols // 2), bf16),
            pltpu.VMEM((n * text, qcols // 2), bf16),
            pltpu.VMEM((text * qcols // HEAD_SIZE, HEAD_SIZE), bf16),
            pltpu.VMEM(residual.shape, bf16),
            pltpu.VMEM(residual.shape, bf16),
            pltpu.VMEM(part, jnp.float32),
            pltpu.VMEM(part, jnp.float32),
            pltpu.VMEM(part, jnp.float32),
            pltpu.VMEM(part, bf16),
            pltpu.VMEM(part, bf16),
            pltpu.SemaphoreType.DMA((4 + n // 2,)),
            hops, hops, steps, steps, steps, steps, steps, steps,
            pltpu.SemaphoreType.DMA,
            pltpu.SemaphoreType.DMA,
            pltpu.SemaphoreType.DMA((n // 2 + 2,)),
            pltpu.SemaphoreType.DMA((n // 2 + 2,)),
            pltpu.SemaphoreType.DMA((n // 2,)),
            pltpu.SemaphoreType.DMA((n // 2,)),
        ]
    return pl.pallas_call(
        run,
        out_shape=jax.ShapeDtypeStruct(residual.shape, residual.dtype),
        in_specs=[hbm] * 9 if middle else [vmem, hbm, hbm, hbm, hbm, vmem, vmem, vmem, vmem],
        out_specs=vmem,
        scratch_shapes=scratch,
        compiler_params=pltpu.CompilerParams(
            collective_id=0, has_side_effects=True, vmem_limit_bytes=60 * 1024 * 1024
        ),
    )(
        queries, vision, key_matrix, value_matrix, out_weight, residual,
        query_norm_gain.reshape(1, HEAD_SIZE), key_norm_gain.reshape(1, HEAD_SIZE),
        attn_gate.reshape(1, 1),
    )


def solution(mesh):
    in_specs = (
        P(("groups", "seq"), "head"),
        P(("groups", "seq"), None),
        P("seq", "head"),
        P("seq", "head"),
        P("head", "seq"),
        P(("groups", "head"), "seq"),
        P(),
        P(),
        P(),
    )
    out_specs = P(("groups", "head"), "seq")
    n = mesh.shape["seq"]
    pairs = mesh.shape["groups"] % 2 == 0
    local = functools.partial(body, n, ring_columns(mesh), pairs)
    return jax.shard_map(local, mesh=mesh, in_specs=in_specs, out_specs=out_specs, check_vma=False)
```

```python
import functools

import jax
import jax.numpy as jnp
from jax import lax
from jax.experimental import pallas as pl
from jax.experimental.pallas import tpu as pltpu
from jax.sharding import PartitionSpec as P

HEAD_SIZE = 128
EPSILON = 1e-05
MESH = pl.DeviceIdType.MESH


def ring_columns(mesh):
    line = mesh.devices[0, :, 0]
    coords = [getattr(d, "coords", None) for d in line]
    if any(c is None for c in coords):
        return 1
    n = len(coords)

    def hops(order):
        return sum(
            sum(abs(a - b) for a, b in zip(coords[order[i]], coords[order[(i + 1) % n]]))
            for i in range(n)
        )

    straight = list(range(n))
    folded = straight[0::2] + straight[1::2][::-1]
    return 2 if n % 4 == 0 and hops(folded) < hops(straight) else 1


def line_split(rows, pairs):
    shared = rows * 19 // 40 // 16 * 16 if pairs else 0
    return shared, rows - shared


def norm(x, gain):
    return x * lax.rsqrt(jnp.mean(x * x, axis=-1, keepdims=True) + EPSILON) * gain


def kernel(
    n, folds, pairs,
    q_ref, vision_ref, key_ref, value_ref, out_w_ref, res_ref, qgain_ref, kgain_ref, gate_ref,
    out_ref,
    wk, wv, vis, ow, kbuf, vbuf, a0, a1, qs, pout, pin, kown, kout, kin, vout, vin,
    load_sem, wsend, wrecv, xsend, xrecv, ksend, krecv, asend, arecv, psend, precv,
    ysend, yrecv, csend, crecv,
):
    group = lax.axis_index("groups")
    me = lax.axis_index("seq")
    head = lax.axis_index("head")
    half = n // folds

    def position(i):
        if folds == 1:
            return i
        z, y = i // 2, i % 2
        return z * (1 - y) + (n - 1 - z) * y

    def index(p):
        if folds == 1:
            return p
        y = p // half
        z = p * (1 - y) + (n - 1 - p) * y
        return z * 2 + y

    pos = position(me)

    def at(offset):
        return index(lax.rem(pos + (n + offset), n))

    neighbours = {1: at(1), -1: at(-1)}
    streams = [(1, 0, n // 2), (-1, 1, n // 2), (1, 1, n // 2 - 1), (-1, 0, n // 2 - 1)]

    def piece(view, send, recv, t, s, received):
        direction, b, _ = streams[t]
        owner = at(-direction * (s + received))
        v = view(b, owner)
        return pltpu.make_async_remote_copy(
            src_ref=v, dst_ref=v, send_sem=send.at[t, s], recv_sem=recv.at[t, s],
            device_id={"seq": neighbours[direction]}, device_id_type=MESH,
        )

    def begin(view, send, recv, b):
        for t, stream in enumerate(streams):
            if stream[1] == b and stream[2] > 0:
                piece(view, send, recv, t, 0, 0).start()

    def run(view, send, recv, arrived=None):
        for s in range(n // 2):
            for t, stream in enumerate(streams):
                if s < stream[2]:
                    piece(view, send, recv, t, s, 1).wait_recv()
                    if s + 1 < stream[2]:
                        piece(view, send, recv, t, s + 1, 0).start()
                    if arrived is not None:
                        arrived(t, s)

    def drain(view, send, recv):
        for t, stream in enumerate(streams):
            for s in range(stream[2]):
                piece(view, send, recv, t, s, 0).wait_send()

    rows = key_ref.shape[0]
    vrows, width = vision_ref.shape
    text = q_ref.shape[0]
    kv_local = key_ref.shape[1] // HEAD_SIZE
    heads_local = q_ref.shape[1] // HEAD_SIZE
    per_group = heads_local // kv_local
    odd = group % 2
    partner = group + 1 - 2 * odd
    weights = (wk, wv)
    mine = pl.ds(pl.multiple_of(me * vrows, 16), vrows)
    bufs = (kbuf, vbuf)
    barrier = pltpu.get_barrier_semaphore()

    def greet(**target):
        pl.semaphore_signal(barrier, inc=1, device_id=target, device_id_type=MESH)

    def kv_view(b, owner):
        return bufs[b].at[pl.ds(pl.multiple_of(owner * vrows, 16), vrows)]

    def queries():
        for h in range(heads_local):
            x = q_ref[:, h * HEAD_SIZE:(h + 1) * HEAD_SIZE].astype(jnp.float32)
            qs[h * text:(h + 1) * text, :] = norm(x, qgain_ref[...]).astype(jnp.bfloat16)

    def store_keys(keys):
        for g in range(kv_local):
            cols = slice(g * HEAD_SIZE, (g + 1) * HEAD_SIZE)
            kbuf[mine, cols] = norm(keys[:, cols], kgain_ref[...]).astype(jnp.bfloat16)

    def line_phase():
        nz = half
        z, y = me // 2, me % 2
        other = z * 2 + 1 - y
        padded = wk.shape[0] // nz
        lead = y * (padded - rows)
        shared, ringed = line_split(rows, pairs)
        middle = ringed - shared

        def slot(b, zz, start, size):
            at_row = pl.multiple_of(zz * padded + lead + start, 16)
            return weights[b].at[pl.ds(at_row, size)]

        parts = [(odd * ringed, shared), (shared, middle)] if pairs else [(0, rows)]
        loads = [
            pltpu.make_async_copy(key_ref, slot(0, z, 0, rows), load_sem.at[0]),
            pltpu.make_async_copy(value_ref, slot(1, z, 0, rows), load_sem.at[1]),
            pltpu.make_async_copy(out_w_ref, ow, load_sem.at[3]),
        ]
        for zz in range(nz):
            column = pl.multiple_of(zz * 2 * rows + y * (2 * rows - padded), HEAD_SIZE)
            loads.append(pltpu.make_async_copy(
                vision_ref.at[:, pl.ds(column, padded)],
                vis.at[:vrows, zz * padded:(zz + 1) * padded], load_sem.at[4 + zz],
            ))
        loads[0].start()
        loads[1].start()
        greet(seq=other)
        greet(head=1 - head)
        if pairs:
            greet(groups=partner)

        @pl.when(z > 0)
        def _():
            greet(seq=(z - 1) * 2 + y)

        @pl.when(z < nz - 1)
        def _():
            greet(seq=(z + 1) * 2 + y)

        if padded > rows:
            for zz in range(nz):
                for w in weights:
                    start = pl.multiple_of(zz * padded + (1 - y) * rows, 16)
                    w[pl.ds(start, padded - rows), :] = jnp.zeros(
                        (padded - rows, w.shape[1]), w.dtype)

        peers = (3 if pairs else 2) + (z + nz - 1) // nz + (2 * nz - 2 - z) // nz
        pl.semaphore_wait(barrier, peers)

        def hop(b, d, s, part, zz):
            start, size = parts[part]
            v = slot(b, zz, start, size)
            k = (b * 2 + (d + 1) // 2) * 2 + part
            return pltpu.make_async_remote_copy(
                src_ref=v, dst_ref=v, send_sem=wsend.at[k, s], recv_sem=wrecv.at[k, s],
                device_id={"seq": (z + d) * 2 + y}, device_id_type=MESH,
            )

        def cross(b, d, s, zz, received):
            which = (1 - odd) if received else odd
            v = slot(b, zz, which * ringed, shared)
            k = b * 2 + (d + 1) // 2
            return pltpu.make_async_remote_copy(
                src_ref=v, dst_ref=v, send_sem=xsend.at[k, s], recv_sem=xrecv.at[k, s],
                device_id={"groups": partner}, device_id_type=MESH,
            )

        def can_send(d, s):
            ahead = (z < nz - 1) if d == 1 else (z > 0)
            behind = (z >= s) if d == 1 else (z + s <= nz - 1)
            return jnp.logical_and(ahead, behind)

        def gets(d, s):
            return (z > s) if d == 1 else (z + s < nz - 1)

        half_rows = vrows // 2

        def vision_out(zz):
            r = pl.ds(pl.multiple_of(head * half_rows, 16), half_rows)
            column = pl.multiple_of(zz * 2 * rows + (1 - y) * (2 * rows - padded), HEAD_SIZE)
            to = pl.ds(pl.multiple_of(vrows + head * half_rows, 16), half_rows)
            return pltpu.make_async_remote_copy(
                src_ref=vision_ref.at[r, pl.ds(column, padded)],
                dst_ref=vis.at[to, zz * padded:(zz + 1) * padded],
                send_sem=ysend.at[zz], recv_sem=yrecv.at[zz],
                device_id={"seq": other}, device_id_type=MESH,
            )

        def vision_pass(zz, received):
            which = (1 - head) if received else head
            r = pl.ds(pl.multiple_of(vrows + which * half_rows, 16), half_rows)
            v = vis.at[r, zz * padded:(zz + 1) * padded]
            return pltpu.make_async_remote_copy(
                src_ref=v, dst_ref=v, send_sem=csend.at[zz], recv_sem=crecv.at[zz],
                device_id={"head": 1 - head}, device_id_type=MESH,
            )

        def begin_line(b):
            loads[b].wait()
            for d in (1, -1):
                @pl.when(can_send(d, 0))
                def _():
                    for part in range(len(parts)):
                        hop(b, d, 0, part, z).start()

        def step(b, s):
            for part in range(len(parts)):
                for d in (1, -1):
                    zz = z - d * (s + 1)

                    @pl.when(gets(d, s))
                    def _():
                        hop(b, d, s, part, zz).wait_recv()
                        if s + 1 < nz - 1:
                            @pl.when(can_send(d, s + 1))
                            def _():
                                hop(b, d, s + 1, part, zz).start()
                        if part == 0 and pairs:
                            cross(b, d, s, zz, False).start()

        def finish(b):
            if pairs:
                for s in range(nz - 1):
                    for d in (1, -1):
                        @pl.when(gets(d, s))
                        def _():
                            cross(b, d, s, z - d * (s + 1), True).wait_recv()

        def give(b):
            src, dst = ((kout, kin), (vout, vin))[b]
            return pltpu.make_async_remote_copy(
                src_ref=src, dst_ref=dst, send_sem=ysend.at[nz + b], recv_sem=yrecv.at[nz + b],
                device_id={"seq": other}, device_id_type=MESH,
            )

        def product(b, first):
            r = slice(0, vrows) if first else slice(vrows, 2 * vrows)
            return jnp.dot(vis[r, :], weights[b][...], preferred_element_type=jnp.float32)

        begin_line(0)
        for zz in range(nz):
            vision_out(zz).start()
        for load in loads[2:]:
            load.start()
        queries()
        for s in range(nz - 1):
            step(0, s)
        begin_line(1)
        finish(0)
        for s in range(nz - 1):
            if s == nz - 2:
                for load in loads[3:]:
                    load.wait()
                for zz in range(nz):
                    vision_out(zz).wait_recv()
                    vision_pass(zz, False).start()
                for zz in range(nz):
                    vision_pass(zz, True).wait_recv()
                kout[...] = product(0, False)
                give(0).start()
                kown[...] = product(0, True)
            step(1, s)
        give(0).wait_recv()
        store_keys(kown[...] + kin[...])
        begin(kv_view, ksend, krecv, 0)
        finish(1)
        vout[...] = product(1, False).astype(vout.dtype)
        give(1).start()
        values = product(1, True)
        give(1).wait_recv()
        vbuf[mine, :] = (values + vin[...].astype(jnp.float32)).astype(jnp.bfloat16)
        begin(kv_view, ksend, krecv, 1)

        def settle():
            for b in range(2):
                give(b).wait_send()
                for s in range(nz - 1):
                    for d in (1, -1):
                        @pl.when(can_send(d, s))
                        def _():
                            for part in range(len(parts)):
                                hop(b, d, s, part, z - d * s).wait_send()

                        if pairs:
                            @pl.when(gets(d, s))
                            def _():
                                cross(b, d, s, z - d * (s + 1), False).wait_send()
            for zz in range(nz):
                vision_out(zz).wait_send()
                vision_pass(zz, False).wait_send()

        return loads[2], settle

    def ring_phase():
        own = pl.ds(pl.multiple_of(me * rows, 16), rows)
        loads = [
            pltpu.make_async_copy(key_ref, wk.at[own], load_sem.at[0]),
            pltpu.make_async_copy(value_ref, wv.at[own], load_sem.at[1]),
            pltpu.make_async_copy(vision_ref, vis, load_sem.at[2]),
            pltpu.make_async_copy(out_w_ref, ow, load_sem.at[3]),
        ]
        for load in loads:
            load.start()
        for target in neighbours.values():
            greet(seq=target)
        greet(head=1 - head)
        if pairs:
            greet(groups=partner)
        pl.semaphore_wait(barrier, 4 if pairs else 3)
        loads[0].wait()
        loads[1].wait()
        shared = (rows * 3 // 10 + 15) // 16 * 16 if pairs else 0
        ringed = rows - shared

        def weight_view(b, owner):
            start = owner * rows
            if pairs:
                start = start + odd * shared
            return weights[b].at[pl.ds(pl.multiple_of(start, 16), ringed)]

        def cross(t, s, received):
            direction, b, _ = streams[t]
            owner = at(-direction * (s + 1))
            which = (1 - odd) if received else odd
            start = owner * rows + which * ringed
            v = weights[b].at[pl.ds(pl.multiple_of(start, 16), shared)]
            return pltpu.make_async_remote_copy(
                src_ref=v, dst_ref=v, send_sem=xsend.at[t, s], recv_sem=xrecv.at[t, s],
                device_id={"groups": partner}, device_id_type=MESH,
            )

        begin(weight_view, wsend, wrecv, 0)
        begin(weight_view, wsend, wrecv, 1)
        queries()
        run(weight_view, wsend, wrecv,
            (lambda t, s: cross(t, s, False).start()) if pairs else None)
        if pairs:
            for t, stream in enumerate(streams):
                for s in range(stream[2]):
                    cross(t, s, True).wait_recv()
        loads[2].wait()
        store_keys(jnp.dot(vis[...], wk[...], preferred_element_type=jnp.float32))
        begin(kv_view, ksend, krecv, 0)
        values = jnp.dot(vis[...], wv[...], preferred_element_type=jnp.float32)
        vbuf[mine, :] = values.astype(jnp.bfloat16)
        begin(kv_view, ksend, krecv, 1)

        def settle():
            drain(weight_view, wsend, wrecv)
            if pairs:
                for t, stream in enumerate(streams):
                    for s in range(stream[2]):
                        cross(t, s, False).wait_send()

        return loads[3], settle

    out_load, settle = (line_phase if folds == 2 else ring_phase)()
    run(kv_view, ksend, krecv)

    total = kbuf.shape[0]
    block = min(total, 2048)
    scale = HEAD_SIZE ** (-0.5)
    attended = (a0, a1)
    mine_text = pl.ds(pl.multiple_of(me * text, 16), text)

    def text_view(b, owner):
        return attended[b].at[pl.ds(pl.multiple_of(owner * text, 16), text)]

    groups_per_buffer = kv_local // 2
    for g in range(kv_local):
        cols = slice(g * HEAD_SIZE, (g + 1) * HEAD_SIZE)
        q = qs[g * per_group * text:(g + 1) * per_group * text, :]
        top = None
        for r in range(0, total, block):
            scores = lax.dot_general(
                q, kbuf[r:r + block, cols], (((1,), (1,)), ((), ())),
                preferred_element_type=jnp.float32,
            ) * scale
            high = jnp.max(scores, axis=-1, keepdims=True)
            new = high if top is None else jnp.maximum(top, high)
            weight = jnp.exp(scores - new)
            part = jnp.sum(weight, axis=-1, keepdims=True)
            product = jnp.dot(
                weight.astype(jnp.bfloat16), vbuf[r:r + block, cols],
                preferred_element_type=jnp.float32,
            )
            if top is None:
                den, num = part, product
            else:
                rescale = jnp.exp(top - new)
                den, num = den * rescale + part, num * rescale + product
            top = new
        result = (num / den).astype(jnp.bfloat16)
        b, inner = g // groups_per_buffer, g % groups_per_buffer
        for h in range(per_group):
            column = (inner * per_group + h) * HEAD_SIZE
            attended[b][mine_text, column:column + HEAD_SIZE] = result[h * text:(h + 1) * text, :]
        if inner == groups_per_buffer - 1:
            begin(text_view, asend, arecv, b)
    run(text_view, asend, arecv)
    out_load.wait()

    out_rows = out_ref.shape[0]
    depth = a0.shape[1]

    def project(which):
        r = pl.ds(pl.multiple_of(which * out_rows, 16), out_rows)
        return jnp.dot(
            a0[r, :], ow[:depth, :], preferred_element_type=jnp.float32
        ) + jnp.dot(a1[r, :], ow[depth:, :], preferred_element_type=jnp.float32)

    pout[...] = project(1 - head).astype(jnp.bfloat16)
    swap = pltpu.make_async_remote_copy(
        src_ref=pout, dst_ref=pin, send_sem=psend, recv_sem=precv,
        device_id={"head": 1 - head}, device_id_type=MESH,
    )
    swap.start()
    projected = project(head)
    swap.wait_recv()
    out_ref[...] = (
        res_ref[...].astype(jnp.float32)
        + jnp.tanh(gate_ref[...]) * (projected + pin[...].astype(jnp.float32))
    ).astype(out_ref.dtype)

    swap.wait_send()
    settle()
    drain(kv_view, ksend, krecv)
    drain(text_view, asend, arecv)


def line_kernel(
    n, cuts, extra, offload,
    q_arg, vision_ref, key_ref, value_ref, out_w_ref, res_arg, qgain_arg, kgain_arg, gate_arg,
    out_ref,
    wk, wv, vis, visx, ow, qout, qall, kacc, vacc, kswap, kswap16, vswap, finals, probs, stats, stat_in,
    own_num, rs_out, rs_in, att, total, pout, pin, q_ref, res_ref, qgain_ref, kgain_ref, gate_ref,
    load_sem, send_sem, recv_sem,
):
    group = lax.axis_index("groups")
    me = lax.axis_index("seq")
    head = lax.axis_index("head")
    z, y = me // 2, me % 2
    odd = group % 2
    side = z // 2
    outer = jnp.logical_or(z == 0, z == 3)
    inner = jnp.logical_not(outer)
    pos = {"e": 3 * side, "m": 1 + side, "M": 2 - side, "E": 3 - 3 * side}
    peers = {
        "x": {"groups": group + 1 - 2 * odd}, "y": {"seq": z * 2 + 1 - y}, "h": {"head": 1 - head},
        "e": {"seq": pos["e"] * 2 + y}, "m": {"seq": pos["m"] * 2 + y}, "M": {"seq": pos["M"] * 2 + y},
    }
    rows, cols = key_ref.shape
    vrows = vision_ref.shape[0]
    text = q_arg.shape[0]
    seen = 2 * vrows
    half_rows = vrows // 2
    padded = wk.shape[0] // 4
    lead = y * (padded - rows)
    chunk = rows // cuts
    split = cuts // 2
    per_group = qall.shape[0]
    tokens = n * text // 2
    wide = per_group * HEAD_SIZE
    bf16, f32 = jnp.bfloat16, jnp.float32
    pieces = 8
    width = wide // pieces
    middle = pieces // 2
    group_heads = per_group // pieces
    weights, sources = (wk, wv), (key_ref, value_ref)
    accs, swaps = (kacc, vacc), (kswap, vswap)
    ids = {"to": {}, "from": {}}
    single = {
        "to": ({"out", "qe", "vx", "up"}, {"mid", "in", "fwd", "qm", "vp", "st", "rs", "ax", "ae", "far"}),
        "from": ({"in", "ae"}, {"out", "mid", "fwd", "qe", "qm", "vx", "vp", "up", "st", "rs", "ax", "far"}),
    }

    def near(rel):
        return "n" if rel in ("e", "m") else rel

    def group_of(way, key):
        kind = key[0]
        if kind == "x":
            return "x", key[1], near(key[2])
        if kind == "s":
            halves = way == "from" and key[1] == 1 and key[2] == 0
            return ("far",) if key[2] else ("s", key[1]) + key[3:] * halves
        if kind == "up":
            return key[:2]
        if kind == "vp":
            return ("vp",)
        if way == "from":
            return ("ay", key[1], key[1] * (key[2] // middle)) if kind == "ay" else key
        if kind in ("out", "mid", "fwd"):
            return key[:2]
        if kind == "in":
            return key[:3]
        return (kind,) if kind in ("yv", "yp", "vx", "rs", "ax", "ae", "ay") else key

    def ident(way, group):
        both, roles = ids[way], single[way]
        role = 1 if group[0] in roles[0] else 2 if group[0] in roles[1] else 0
        if group not in both:
            both[group] = role, sum(1 for r, _ in both.values() if r == role)
        role, i = both[group]
        return i if role == 0 else shared[way] + i

    def copy(key, src, dst, to):
        out, into = (ident(way, group_of(way, key)) for way in ("to", "from"))
        return pltpu.make_async_remote_copy(
            src_ref=src, dst_ref=dst, send_sem=send_sem.at[out], recv_sem=recv_sem.at[into],
            device_id=peers[to], device_id_type=MESH,
        )

    def got(key, dst):
        copy(key, dst, dst, "h").wait_recv()

    def sender(log):
        def send(key, view, to):
            src, dst = view() if callable(view) else view
            copy(key, src, dst, to).start()
            log.setdefault(group_of("to", key), []).append(key)
        return send

    def bulk(group, count):
        kind = group[0]
        if kind in ("x", "out", "mid", "in", "fwd"):
            return weights[group[1]].at[pl.ds(0, count * chunk)]
        if kind in ("yv", "yp"):
            return vis.at[pl.ds(0, count * half_rows), pl.ds(0, padded)]
        if kind in ("vx", "vp"):
            return visx.at[pl.ds(0, count * half_rows)]
        if kind in ("s", "far"):
            return swaps[group[1] if kind == "s" else 1].at[0, 0]
        if kind == "up":
            return kswap16.at[0] if group[1] == 0 else vswap.at[2, 0]
        if kind in ("qe", "qm"):
            return qall.at[:, pl.ds(0, 2 * text if kind == "qe" else tokens)]
        if kind == "ax":
            return att.at[0, pl.ds(0, tokens)]
        return {"q": qout, "st": stat_in, "rs": rs_out, "ae": att.at[0], "ay": att.at[0], "p": pout}[kind]

    def drain(log):
        for group, keys in log.items():
            view = bulk(group, len(keys))
            copy(keys[0], view, view, "h").wait_send()

    shared = {"to": 13, "from": 22}
    outer_log, inner_log, log = {}, {}, {}

    def start_of(j, which):
        return j * chunk + which * (rows - chunk - 2 * chunk * j)

    def slot(b, rel, start, size=chunk):
        return weights[b].at[pl.ds(pl.multiple_of(pos[rel] * padded + lead + start, 16), size)]

    def mine(b, rel, j):
        return slot(b, rel, start_of(j, odd))

    def theirs(b, rel, j):
        return slot(b, rel, start_of(j, 1 - odd))

    def source(b, j):
        return sources[b].at[pl.ds(pl.multiple_of(start_of(j, odd), 16), chunk)]

    def column(yy, zz):
        return pl.ds(pl.multiple_of(zz * 2 * rows + yy * (2 * rows - padded), HEAD_SIZE), padded)

    def block(rel):
        return pl.ds(pl.multiple_of(pos[rel] * padded, HEAD_SIZE), padded)

    def part(which, far):
        return pl.ds(pl.multiple_of(far * vrows + which * half_rows, 16), half_rows)

    def lanes(which):
        return pl.ds(pl.multiple_of(which * HEAD_SIZE, HEAD_SIZE), HEAD_SIZE)

    def piece(c):
        return slice(c * width, (c + 1) * width)

    def span(which):
        return pl.ds(pl.multiple_of(which * tokens, 16), tokens)

    def crossed(b, rel, count):
        got(("x", b, rel, 0), slot(b, rel, 0, count * chunk))

    def vision_send(send, i, rel):
        send(("yv", i), lambda: (vision_ref.at[part(head, 0), column(1 - y, pos[rel])],
                                 vis.at[part(head, 1), block(rel)]), "y")

    def vision_pass(send, i, rel):
        got(("yv", i), vis.at[part(head, 1), block(rel)])
        send(("yp", i), lambda: (vis.at[part(head, 1), block(rel)],) * 2, "h")

    def vision_done(i, rel):
        got(("yp", i), vis.at[part(1 - head, 1), block(rel)])

    def give(send, b, x):
        swap = swaps[b]
        swap[x, 0] = accs[b][x, :, lanes(1 - y)].astype(swap.dtype)
        for k in range(2):
            send(("s", b, x, k), lambda k=k: (swap.at[x, 0, pl.ds(k * vrows, vrows)],
                                              swap.at[x, 1, pl.ds((1 - k) * vrows, vrows)]), "y")

    def half(ref, k):
        return ref.at[pl.ds(k * vrows, vrows)]

    def take(b, x):
        if (b, x) == (1, 0):
            for k in range(2):
                got(("s", b, x, k), half(swaps[b].at[x, 1], 1 - k))
        else:
            got(("s", b, x, 0), swaps[b].at[x, 1])
        return accs[b][x, :, lanes(y)] + swaps[b][x, 1].astype(f32)

    def multiply(b, rel, start):
        part = jnp.dot(vis[:, block(rel)], weights[b][block(rel), :], preferred_element_type=f32)
        accs[b][0] = part if start else accs[b][0] + part

    loads = [
        pltpu.make_async_copy(sources[b], weights[b].at[pl.ds(pl.multiple_of(z * padded + lead, 16), rows)], load_sem.at[b])
        for b in range(2)
    ]
    for zz in range(4):
        loads.append(pltpu.make_async_copy(
            vision_ref.at[:, column(y, zz)], vis.at[:vrows, zz * padded:(zz + 1) * padded],
            load_sem.at[2 + zz]))
    out_load = pltpu.make_async_copy(out_w_ref, ow, load_sem.at[6])
    small = [
        pltpu.make_async_copy(src, dst, load_sem.at[7 + i])
        for i, (src, dst) in enumerate([
            (q_arg, q_ref), (qgain_arg, qgain_ref), (kgain_arg, kgain_ref), (gate_arg, gate_ref), (res_arg, res_ref)])
    ]
    for load in small:
        load.start()

    barrier = pltpu.get_barrier_semaphore()

    def greet(to):
        pl.semaphore_signal(barrier, inc=1, device_id=peers[to], device_id_type=MESH)

    greet("y")
    greet("h")
    greet("x")

    @pl.when(outer)
    def _():
        greet("m")
        pl.semaphore_wait(barrier, 4)

    @pl.when(inner)
    def _():
        greet("e")
        greet("M")
        pl.semaphore_wait(barrier, 5)

    first = split + extra
    order_e = ("E", "e", "m", "M")
    order_m = ("m", "e", "M", "E")
    inward = (("m", "M", "E"), ("m", "M") if offload else ("m", "M", "E"))

    @pl.when(outer)
    def _():
        send = sender(outer_log)
        for j in range(first):
            send(("out", 0, j), lambda j=j: (source(0, j), mine(0, "e", j)), "m")
        vision_send(send, 0, order_e[0])

    @pl.when(inner)
    def _():
        send = sender(inner_log)
        for j in range(split):
            send(("mid", 0, j), lambda j=j: (source(0, j), mine(0, "m", j)), "M")
            send(("in", 0, "m", j), lambda j=j: (source(0, j), mine(0, "m", j)), "e")
        vision_send(send, 0, order_m[0])

    for load in loads:
        load.start()
    out_load.start()
    for w in weights:
        for zz in range(4):
            at = pl.multiple_of(zz * padded + (1 - y) * rows, 16)
            w[pl.ds(at, padded - rows), :] = jnp.zeros((padded - rows, cols), w.dtype)

    for load in small:
        load.wait()
    own_tokens = pl.ds(pl.multiple_of(me * text, 16), text)
    far_tokens = pl.ds(pl.multiple_of((z * 2 + 1 - y) * text, 16), text)
    for h in range(per_group):
        for which in (1 - y, y):
            at = pl.ds(pl.multiple_of(which * wide + h * HEAD_SIZE, HEAD_SIZE), HEAD_SIZE)
            value = norm(q_ref[:, at].astype(f32), qgain_ref[...]).astype(bf16)
            if which is y:
                qall[h, own_tokens, :] = value
            else:
                qout[h] = value
    sender(log)(("q",), lambda: (qout, qall.at[:, own_tokens, :]), "y")

    def line_tokens(zz):
        return qall.at[:, pl.ds(pl.multiple_of(zz * 2 * text, 16), 2 * text), :]

    def side_tokens(which):
        return qall.at[:, span(which), :]

    @pl.when(outer)
    def _():
        send = sender(outer_log)
        for i in range(1, 4):
            vision_send(send, i, order_e[i])

        def inbound(b, rel):
            for j in range(split):
                got(("in", b, rel, j), mine(b, rel, j))
                send(("x", b, rel, j), lambda b=b, rel=rel, j=j: (mine(b, rel, j),) * 2, "x")

        for j in range(first):
            send(("out", 1, j), lambda j=j: (source(1, j), mine(1, "e", j)), "m")
        inbound(0, "m")
        got(("q",), qall.at[:, far_tokens, :])
        send(("qe",), lambda: (line_tokens(z), line_tokens(z)), "m")
        if offload:
            send(("vx", 0), lambda: (vision_ref.at[part(head, 0), column(y, pos["E"])],
                                     visx.at[part(head, 0)]), "m")
        vision_pass(send, 0, "E")
        if offload:
            send(("vx", 1), lambda: (vis.at[part(head, 1), block("E")], visx.at[part(head, 1)]), "m")
        inbound(0, "M")
        vision_pass(send, 1, "e")
        inbound(0, "E")
        vision_pass(send, 2, "m")
        for load in loads:
            load.wait()
        vision_done(1, "e")
        multiply(0, "e", True)
        inbound(1, "m")
        for i, rel in ((0, "E"), (2, "m")):
            vision_done(i, rel)
            crossed(0, rel, split)
            multiply(0, rel, False)
        vision_pass(send, 3, "M")
        for rel in inward[1][1:]:
            inbound(1, rel)
        crossed(0, "M", split)
        vision_done(3, "M")
        multiply(0, "M", False)
        give(send, 0, 0)
        multiply(1, "e", True)
        crossed(1, "m", split)
        multiply(1, "m", False)
        for rel in inward[1][1:]:
            crossed(1, rel, split)
            multiply(1, rel, False)
        give(send, 1, 0)
        kswap16[0] = norm(take(0, 0), kgain_ref[...]).astype(bf16)
        send(("up", 0), lambda: (kswap16.at[0], kswap16.at[1]), "m")
        for k in range(2):
            got(("s", 1, 0, k), half(vswap.at[0, 1], 1 - k))
            here = slice((1 - k) * vrows, (2 - k) * vrows)
            vswap[2, 0, here] = (vacc[0, here, lanes(y)] + vswap[0, 1, here].astype(f32)).astype(bf16)
            send(("up", 1, k), (half(vswap.at[2, 0], 1 - k), half(vswap.at[2, 1], 1 - k)), "m")

    @pl.when(inner)
    def _():
        send = sender(inner_log)
        for i in range(1, 4):
            vision_send(send, i, order_m[i])


        def from_end(b, j):
            got(("out", b, j), mine(b, "e", j))
            if j < split:
                send(("fwd", b, j), lambda: (mine(b, "e", j),) * 2, "M")
            if j < cuts - first:
                send(("x", b, "e", j), lambda: (mine(b, "e", j),) * 2, "x")

        def from_middle(b, j):
            got(("mid", b, j), mine(b, "M", j))
            send(("in", b, "M", j), lambda: (mine(b, "M", j),) * 2, "e")
            send(("x", b, "M", j), lambda: (mine(b, "M", j),) * 2, "x")

        def from_far_end(b, j):
            got(("fwd", b, j), mine(b, "E", j))
            if "E" in inward[b]:
                send(("in", b, "E", j), lambda: (mine(b, "E", j),) * 2, "e")
            send(("x", b, "E", j), lambda: (mine(b, "E", j),) * 2, "x")

        for j in range(first):
            from_end(0, j)
            if j < split:
                from_middle(0, j)
        for j in range(split):
            from_far_end(0, j)
        for j in range(split):
            send(("in", 1, "m", j), lambda j=j: (source(1, j), mine(1, "m", j)), "e")
        vision_pass(send, 0, "m")
        for j in range(first):
            from_end(1, j)
        for j in range(split):
            send(("mid", 1, j), lambda j=j: (source(1, j), mine(1, "m", j)), "M")
        got(("q",), qall.at[:, far_tokens, :])
        vision_pass(send, 1, "e")
        for load in loads:
            load.wait()
        vision_done(0, "m")
        multiply(0, "m", True)
        for j in range(split):
            from_far_end(1, j)
        got(("qe",), line_tokens(pos["e"]))
        send(("qm",), lambda: (side_tokens(side),) * 2, "M")
        for j in range(split):
            from_middle(1, j)
        vision_pass(send, 2, "M")
        vision_done(1, "e")
        crossed(0, "e", cuts - first)
        multiply(0, "e", False)
        vision_done(2, "M")
        crossed(0, "M", split)
        multiply(0, "M", False)
        vision_pass(send, 3, "E")
        crossed(0, "E", split)
        vision_done(3, "E")
        multiply(0, "E", False)
        give(send, 0, 0)
        multiply(1, "m", True)
        crossed(1, "e", cuts - first)
        multiply(1, "e", False)
        crossed(1, "E", split)
        multiply(1, "E", False)
        if offload:
            for k in range(2):
                got(("vx", k), visx.at[part(head, k)])
                send(("vp", k), lambda k=k: (visx.at[part(head, k)],) * 2, "h")
            got(("vp", 0), visx.at[pl.ds(0, vrows)])
            vacc[1] = jnp.dot(visx[...], wv[block("E"), :], preferred_element_type=f32)
            give(send, 1, 1)
        crossed(1, "M", split)
        multiply(1, "M", False)
        give(send, 1, 0)
        got(("qm",), side_tokens(1 - side))

        lane = lax.broadcasted_iota(jnp.int32, (2 * tokens, HEAD_SIZE), 1)
        scale = HEAD_SIZE ** (-0.5)

        def score(r):
            k = finals[0, r * seen:(r + 1) * seen, :]
            tops = jnp.zeros((2 * tokens, HEAD_SIZE), f32)
            dens = jnp.ones((2 * tokens, HEAD_SIZE), f32)
            for h in range(per_group):
                s = lax.dot_general(
                    qall[h], k, (((1,), (1,)), ((), ())), preferred_element_type=f32) * scale
                top = jnp.max(s, axis=-1, keepdims=True)
                p = jnp.exp(s - top)
                den = jnp.sum(p, axis=-1, keepdims=True)
                probs[h, :, r * seen:(r + 1) * seen] = p.astype(bf16)
                tops = jnp.where(lane == h, top, tops)
                dens = jnp.where(lane == h, den, dens)
            stats[r, 0] = tops
            stats[r, 1] = dens

        finals[0, :seen, :] = norm(take(0, 0), kgain_ref[...]).astype(bf16)
        score(0)
        got(("up", 0), kswap16.at[1])
        finals[0, seen:, :] = kswap16[1]
        score(1)

        def merge(top_a, den_a, top_b, den_b):
            top = jnp.maximum(top_a, top_b)
            fa, fb = jnp.exp(top_a - top), jnp.exp(top_b - top)
            return top, fa * den_a + fb * den_b, fa, fb

        top, den, f0, f1 = merge(stats[0, 0], stats[0, 1], stats[1, 0], stats[1, 1])
        stats[0, 0] = f0
        stats[1, 0] = f1
        stats[2, 0] = top
        stats[2, 1] = den
        send(("st",), lambda: (stats.at[2, :, span(1 - side)], stat_in), "M")

        finals[1, :seen, :] = take(1, 0).astype(bf16)
        far_values = take(1, 1) if offload else 0.0
        got(("up", 1), vswap.at[2, 1])
        finals[1, seen:, :] = (far_values + vswap[2, 1].astype(f32)).astype(bf16)
        got(("st",), stat_in)
        _, den, fs, fo = merge(stats[2, 0, span(side), :], stats[2, 1, span(side), :], stat_in[0], stat_in[1])
        inverse = 1.0 / den
        other = fo * inverse
        mine0 = fs * inverse * stats[0, 0, span(side), :]
        mine1 = fs * inverse * stats[1, 0, span(side), :]
        far0, far1 = stats[0, 0, span(1 - side), :], stats[1, 0, span(1 - side), :]

        def numerator(h, which, c0, c1):
            p = probs[h, span(which), :]
            return (c0[:, h:h + 1] * jnp.dot(p[:, :seen], finals[1, :seen, :], preferred_element_type=f32)
                    + c1[:, h:h + 1] * jnp.dot(p[:, seen:], finals[1, seen:, :], preferred_element_type=f32))


        for c in range(pieces):
            for h in range(c * group_heads, (c + 1) * group_heads):
                rs_out[:, h * HEAD_SIZE:(h + 1) * HEAD_SIZE] = numerator(h, 1 - side, far0, far1).astype(bf16)
            send(("rs", c), lambda c=c: (rs_out.at[:, piece(c)], rs_in.at[:, piece(c)]), "M")
        for h in range(per_group):
            own_num[:, h * HEAD_SIZE:(h + 1) * HEAD_SIZE] = numerator(h, side, mine0, mine1)
        for c in range(pieces):
            got(("rs", c), rs_in.at[:, piece(c)])
            for h in range(c * group_heads, (c + 1) * group_heads):
                at = slice(h * HEAD_SIZE, (h + 1) * HEAD_SIZE)
                att[y, span(side), at] = (
                    own_num[:, at] + other[:, h:h + 1] * rs_in[:, at].astype(f32)).astype(bf16)
            here = lambda c=c: (att.at[y, span(side), piece(c)],) * 2
            send(("ax", c), here, "M")
            send(("ae", 0, c), here, "e")
            send(("ay", 0, c), here, "y")

    out_load.wait()

    def forward(t, c):
        view = lambda: (att.at[y, span(side if t == 0 else 1 - side), piece(c)],) * 2

        @pl.when(outer)
        def _():
            got(("ae", t, c), view()[0])
            sender(outer_log)(("ay", t, c), view, "y")

        if t == 1:
            @pl.when(inner)
            def _():
                send = sender(inner_log)
                got(("ax", c), view()[0])
                send(("ae", 1, c), view, "e")
                send(("ay", 1, c), view, "y")

    def project(t, which, start, stop):
        if which is not y:
            got(("ay", t, start), att.at[
                which, span(side if t == 0 else 1 - side), start * width:stop * width])
        depth = (stop - start) * width
        part = jnp.dot(
            att[which, span(side if t == 0 else 1 - side), start * width:stop * width],
            ow[pl.ds(pl.multiple_of(which * wide + start * width, 16), depth), :],
            preferred_element_type=f32)
        total[t] = part if which is y and start == 0 else total[t] + part

    def settle(t):
        which = side if t == 0 else 1 - side

        @pl.when(which != head)
        def _():
            pout[...] = total[t].astype(bf16)
            copy(("p",), pout, pin, "h").start()

    other = 1 - y
    for c in range(pieces):
        forward(0, c)
    project(0, y, 0, pieces)
    for c in range(middle):
        forward(1, c)
    project(0, other, 0, pieces)
    settle(0)
    for c in range(middle, pieces):
        forward(1, c)
    project(1, y, 0, pieces)
    project(1, other, 0, middle)
    project(1, other, middle, pieces)
    settle(1)
    mine_first = side == head
    projected = jnp.where(mine_first, total[0], total[1])
    got(("p",), pin)
    out_ref[...] = (
        res_ref[...].astype(f32)
        + jnp.tanh(gate_ref[...]) * (projected + pin[...].astype(f32))
    ).astype(out_ref.dtype)
    log["p",] = [("p",)]

    @pl.when(outer)
    def _():
        drain(outer_log)

    @pl.when(inner)
    def _():
        drain(inner_log)

    drain(log)
    for way, sem in (("to", send_sem), ("from", recv_sem)):
        counts = [sum(1 for r, _ in ids[way].values() if r == role) for role in range(3)]
        assert counts[0] == shared[way] and sem.shape[0] == counts[0] + max(counts[1:]), (way, counts, sem.shape)


def line_call(n, queries, vision, key_matrix, value_matrix, out_weight, residual):
    rows, columns = key_matrix.shape
    vrows = vision.shape[0]
    text, qcols = queries.shape
    bf16, f32 = jnp.bfloat16, jnp.float32
    padded = -(-rows // HEAD_SIZE) * HEAD_SIZE
    per_group = qcols // HEAD_SIZE // 2
    tokens = n * text // 2
    seen = 2 * vrows
    scratch = [
        pltpu.VMEM((4 * padded, columns), bf16),
        pltpu.VMEM((4 * padded, columns), bf16),
        pltpu.VMEM((seen, 4 * padded), bf16),
        pltpu.VMEM((seen, padded), bf16),
        pltpu.VMEM(out_weight.shape, bf16),
        pltpu.VMEM((per_group, text, HEAD_SIZE), bf16),
        pltpu.VMEM((per_group, 2 * tokens, HEAD_SIZE), bf16),
        pltpu.VMEM((1, seen, columns), f32),
        pltpu.VMEM((2, seen, columns), f32),
        pltpu.VMEM((1, 2, seen, HEAD_SIZE), f32),
        pltpu.VMEM((2, seen, HEAD_SIZE), bf16),
        pltpu.VMEM((3, 2, seen, HEAD_SIZE), bf16),
        pltpu.VMEM((2, 2 * seen, HEAD_SIZE), bf16),
        pltpu.VMEM((per_group, 2 * tokens, 2 * seen), bf16),
        pltpu.VMEM((3, 2, 2 * tokens, HEAD_SIZE), f32),
        pltpu.VMEM((2, tokens, HEAD_SIZE), f32),
        pltpu.VMEM((tokens, qcols // 2), f32),
        pltpu.VMEM((tokens, qcols // 2), bf16),
        pltpu.VMEM((tokens, qcols // 2), bf16),
        pltpu.VMEM((2, 2 * tokens, qcols // 2), bf16),
        pltpu.VMEM((2,) + residual.shape, f32),
        pltpu.VMEM(residual.shape, bf16),
        pltpu.VMEM(residual.shape, bf16),
        pltpu.VMEM(queries.shape, bf16),
        pltpu.VMEM(residual.shape, bf16),
        pltpu.VMEM((1, HEAD_SIZE), f32),
        pltpu.VMEM((1, HEAD_SIZE), f32),
        pltpu.VMEM((1, 1), f32),
        pltpu.SemaphoreType.DMA((12,)),
        pltpu.SemaphoreType.DMA((29,)),
        pltpu.SemaphoreType.DMA((31 + 6 * (6 // 2) + 2 * 1 + 2 * 8,)),
    ]
    return functools.partial(line_kernel, n, 6, 1, True), scratch


def body(n, folds, pairs, queries, vision, key_matrix, value_matrix, out_weight, residual,
         query_norm_gain, key_norm_gain, attn_gate):
    rows, columns = key_matrix.shape
    vrows, width = vision.shape
    text, qcols = queries.shape
    bf16 = jnp.bfloat16
    vmem = pl.BlockSpec(memory_space=pltpu.VMEM)
    hbm = pl.BlockSpec(memory_space=pl.ANY)
    steps = pltpu.SemaphoreType.DMA((4, n // 2))
    hops = pltpu.SemaphoreType.DMA((8, n // 2))
    if folds == 2:
        depth = n // 2 * (-(-rows // HEAD_SIZE) * HEAD_SIZE)
        seen = (2 * vrows, depth)
        part = (vrows, columns)
    else:
        depth = n * rows
        seen = (vrows, width)
        part = (16, HEAD_SIZE)
    middle = (
        folds == 2 and n == 8 and pairs and columns == 2 * HEAD_SIZE
        and rows % 96 == 0 and qcols % (8 * HEAD_SIZE) == 0
    )
    if middle:
        run, scratch = line_call(n, queries, vision, key_matrix, value_matrix, out_weight, residual)
    else:
        run, scratch = functools.partial(kernel, n, folds, pairs), [
            pltpu.VMEM((depth, columns), bf16),
            pltpu.VMEM((depth, columns), bf16),
            pltpu.VMEM(seen, bf16),
            pltpu.VMEM(out_weight.shape, bf16),
            pltpu.VMEM((n * vrows, columns), bf16),
            pltpu.VMEM((n * vrows, columns), bf16),
            pltpu.VMEM((n * text, qcols // 2), bf16),
            pltpu.VMEM((n * text, qcols // 2), bf16),
            pltpu.VMEM((text * qcols // HEAD_SIZE, HEAD_SIZE), bf16),
            pltpu.VMEM(residual.shape, bf16),
            pltpu.VMEM(residual.shape, bf16),
            pltpu.VMEM(part, jnp.float32),
            pltpu.VMEM(part, jnp.float32),
            pltpu.VMEM(part, jnp.float32),
            pltpu.VMEM(part, bf16),
            pltpu.VMEM(part, bf16),
            pltpu.SemaphoreType.DMA((4 + n // 2,)),
            hops, hops, steps, steps, steps, steps, steps, steps,
            pltpu.SemaphoreType.DMA,
            pltpu.SemaphoreType.DMA,
            pltpu.SemaphoreType.DMA((n // 2 + 2,)),
            pltpu.SemaphoreType.DMA((n // 2 + 2,)),
            pltpu.SemaphoreType.DMA((n // 2,)),
            pltpu.SemaphoreType.DMA((n // 2,)),
        ]
    return pl.pallas_call(
        run,
        out_shape=jax.ShapeDtypeStruct(residual.shape, residual.dtype),
        in_specs=[hbm] * 9 if middle else [vmem, hbm, hbm, hbm, hbm, vmem, vmem, vmem, vmem],
        out_specs=vmem,
        scratch_shapes=scratch,
        compiler_params=pltpu.CompilerParams(
            collective_id=0, has_side_effects=True, vmem_limit_bytes=60 * 1024 * 1024
        ),
    )(
        queries, vision, key_matrix, value_matrix, out_weight, residual,
        query_norm_gain.reshape(1, HEAD_SIZE), key_norm_gain.reshape(1, HEAD_SIZE),
        attn_gate.reshape(1, 1),
    )


def solution(mesh):
    in_specs = (
        P(("groups", "seq"), "head"),
        P(("groups", "seq"), None),
        P("seq", "head"),
        P("seq", "head"),
        P("head", "seq"),
        P(("groups", "head"), "seq"),
        P(),
        P(),
        P(),
    )
    out_specs = P(("groups", "head"), "seq")
    n = mesh.shape["seq"]
    pairs = mesh.shape["groups"] % 2 == 0
    local = functools.partial(body, n, ring_columns(mesh), pairs)
    return jax.shard_map(local, mesh=mesh, in_specs=in_specs, out_specs=out_specs, check_vma=False)
```

```python
import functools

import jax
import jax.numpy as jnp
from jax import lax
from jax.experimental import pallas as pl
from jax.experimental.pallas import tpu as pltpu
from jax.sharding import PartitionSpec as P

HEAD_SIZE = 128
EPSILON = 1e-05
MESH = pl.DeviceIdType.MESH


def ring_columns(mesh):
    line = mesh.devices[0, :, 0]
    coords = [getattr(d, "coords", None) for d in line]
    if any(c is None for c in coords):
        return 1
    n = len(coords)

    def hops(order):
        return sum(
            sum(abs(a - b) for a, b in zip(coords[order[i]], coords[order[(i + 1) % n]]))
            for i in range(n)
        )

    straight = list(range(n))
    folded = straight[0::2] + straight[1::2][::-1]
    return 2 if n % 4 == 0 and hops(folded) < hops(straight) else 1


def line_split(rows, pairs):
    shared = rows * 19 // 40 // 16 * 16 if pairs else 0
    return shared, rows - shared


def norm(x, gain):
    return x * lax.rsqrt(jnp.mean(x * x, axis=-1, keepdims=True) + EPSILON) * gain


def kernel(
    n, folds, pairs,
    q_ref, vision_ref, key_ref, value_ref, out_w_ref, res_ref, qgain_ref, kgain_ref, gate_ref,
    out_ref,
    wk, wv, vis, ow, kbuf, vbuf, a0, a1, qs, pout, pin, kown, kout, kin, vout, vin,
    load_sem, wsend, wrecv, xsend, xrecv, ksend, krecv, asend, arecv, psend, precv,
    ysend, yrecv, csend, crecv,
):
    group = lax.axis_index("groups")
    me = lax.axis_index("seq")
    head = lax.axis_index("head")
    half = n // folds

    def position(i):
        if folds == 1:
            return i
        z, y = i // 2, i % 2
        return z * (1 - y) + (n - 1 - z) * y

    def index(p):
        if folds == 1:
            return p
        y = p // half
        z = p * (1 - y) + (n - 1 - p) * y
        return z * 2 + y

    pos = position(me)

    def at(offset):
        return index(lax.rem(pos + (n + offset), n))

    neighbours = {1: at(1), -1: at(-1)}
    streams = [(1, 0, n // 2), (-1, 1, n // 2), (1, 1, n // 2 - 1), (-1, 0, n // 2 - 1)]

    def piece(view, send, recv, t, s, received):
        direction, b, _ = streams[t]
        owner = at(-direction * (s + received))
        v = view(b, owner)
        return pltpu.make_async_remote_copy(
            src_ref=v, dst_ref=v, send_sem=send.at[t, s], recv_sem=recv.at[t, s],
            device_id={"seq": neighbours[direction]}, device_id_type=MESH,
        )

    def begin(view, send, recv, b):
        for t, stream in enumerate(streams):
            if stream[1] == b and stream[2] > 0:
                piece(view, send, recv, t, 0, 0).start()

    def run(view, send, recv, arrived=None):
        for s in range(n // 2):
            for t, stream in enumerate(streams):
                if s < stream[2]:
                    piece(view, send, recv, t, s, 1).wait_recv()
                    if s + 1 < stream[2]:
                        piece(view, send, recv, t, s + 1, 0).start()
                    if arrived is not None:
                        arrived(t, s)

    def drain(view, send, recv):
        for t, stream in enumerate(streams):
            for s in range(stream[2]):
                piece(view, send, recv, t, s, 0).wait_send()

    rows = key_ref.shape[0]
    vrows, width = vision_ref.shape
    text = q_ref.shape[0]
    kv_local = key_ref.shape[1] // HEAD_SIZE
    heads_local = q_ref.shape[1] // HEAD_SIZE
    per_group = heads_local // kv_local
    odd = group % 2
    partner = group + 1 - 2 * odd
    weights = (wk, wv)
    mine = pl.ds(pl.multiple_of(me * vrows, 16), vrows)
    bufs = (kbuf, vbuf)
    barrier = pltpu.get_barrier_semaphore()

    def greet(**target):
        pl.semaphore_signal(barrier, inc=1, device_id=target, device_id_type=MESH)

    def kv_view(b, owner):
        return bufs[b].at[pl.ds(pl.multiple_of(owner * vrows, 16), vrows)]

    def queries():
        for h in range(heads_local):
            x = q_ref[:, h * HEAD_SIZE:(h + 1) * HEAD_SIZE].astype(jnp.float32)
            qs[h * text:(h + 1) * text, :] = norm(x, qgain_ref[...]).astype(jnp.bfloat16)

    def store_keys(keys):
        for g in range(kv_local):
            cols = slice(g * HEAD_SIZE, (g + 1) * HEAD_SIZE)
            kbuf[mine, cols] = norm(keys[:, cols], kgain_ref[...]).astype(jnp.bfloat16)

    def line_phase():
        nz = half
        z, y = me // 2, me % 2
        other = z * 2 + 1 - y
        padded = wk.shape[0] // nz
        lead = y * (padded - rows)
        shared, ringed = line_split(rows, pairs)
        middle = ringed - shared

        def slot(b, zz, start, size):
            at_row = pl.multiple_of(zz * padded + lead + start, 16)
            return weights[b].at[pl.ds(at_row, size)]

        parts = [(odd * ringed, shared), (shared, middle)] if pairs else [(0, rows)]
        loads = [
            pltpu.make_async_copy(key_ref, slot(0, z, 0, rows), load_sem.at[0]),
            pltpu.make_async_copy(value_ref, slot(1, z, 0, rows), load_sem.at[1]),
            pltpu.make_async_copy(out_w_ref, ow, load_sem.at[3]),
        ]
        for zz in range(nz):
            column = pl.multiple_of(zz * 2 * rows + y * (2 * rows - padded), HEAD_SIZE)
            loads.append(pltpu.make_async_copy(
                vision_ref.at[:, pl.ds(column, padded)],
                vis.at[:vrows, zz * padded:(zz + 1) * padded], load_sem.at[4 + zz],
            ))
        loads[0].start()
        loads[1].start()
        greet(seq=other)
        greet(head=1 - head)
        if pairs:
            greet(groups=partner)

        @pl.when(z > 0)
        def _():
            greet(seq=(z - 1) * 2 + y)

        @pl.when(z < nz - 1)
        def _():
            greet(seq=(z + 1) * 2 + y)

        if padded > rows:
            for zz in range(nz):
                for w in weights:
                    start = pl.multiple_of(zz * padded + (1 - y) * rows, 16)
                    w[pl.ds(start, padded - rows), :] = jnp.zeros(
                        (padded - rows, w.shape[1]), w.dtype)

        peers = (3 if pairs else 2) + (z + nz - 1) // nz + (2 * nz - 2 - z) // nz
        pl.semaphore_wait(barrier, peers)

        def hop(b, d, s, part, zz):
            start, size = parts[part]
            v = slot(b, zz, start, size)
            k = (b * 2 + (d + 1) // 2) * 2 + part
            return pltpu.make_async_remote_copy(
                src_ref=v, dst_ref=v, send_sem=wsend.at[k, s], recv_sem=wrecv.at[k, s],
                device_id={"seq": (z + d) * 2 + y}, device_id_type=MESH,
            )

        def cross(b, d, s, zz, received):
            which = (1 - odd) if received else odd
            v = slot(b, zz, which * ringed, shared)
            k = b * 2 + (d + 1) // 2
            return pltpu.make_async_remote_copy(
                src_ref=v, dst_ref=v, send_sem=xsend.at[k, s], recv_sem=xrecv.at[k, s],
                device_id={"groups": partner}, device_id_type=MESH,
            )

        def can_send(d, s):
            ahead = (z < nz - 1) if d == 1 else (z > 0)
            behind = (z >= s) if d == 1 else (z + s <= nz - 1)
            return jnp.logical_and(ahead, behind)

        def gets(d, s):
            return (z > s) if d == 1 else (z + s < nz - 1)

        half_rows = vrows // 2

        def vision_out(zz):
            r = pl.ds(pl.multiple_of(head * half_rows, 16), half_rows)
            column = pl.multiple_of(zz * 2 * rows + (1 - y) * (2 * rows - padded), HEAD_SIZE)
            to = pl.ds(pl.multiple_of(vrows + head * half_rows, 16), half_rows)
            return pltpu.make_async_remote_copy(
                src_ref=vision_ref.at[r, pl.ds(column, padded)],
                dst_ref=vis.at[to, zz * padded:(zz + 1) * padded],
                send_sem=ysend.at[zz], recv_sem=yrecv.at[zz],
                device_id={"seq": other}, device_id_type=MESH,
            )

        def vision_pass(zz, received):
            which = (1 - head) if received else head
            r = pl.ds(pl.multiple_of(vrows + which * half_rows, 16), half_rows)
            v = vis.at[r, zz * padded:(zz + 1) * padded]
            return pltpu.make_async_remote_copy(
                src_ref=v, dst_ref=v, send_sem=csend.at[zz], recv_sem=crecv.at[zz],
                device_id={"head": 1 - head}, device_id_type=MESH,
            )

        def begin_line(b):
            loads[b].wait()
            for d in (1, -1):
                @pl.when(can_send(d, 0))
                def _():
                    for part in range(len(parts)):
                        hop(b, d, 0, part, z).start()

        def step(b, s):
            for part in range(len(parts)):
                for d in (1, -1):
                    zz = z - d * (s + 1)

                    @pl.when(gets(d, s))
                    def _():
                        hop(b, d, s, part, zz).wait_recv()
                        if s + 1 < nz - 1:
                            @pl.when(can_send(d, s + 1))
                            def _():
                                hop(b, d, s + 1, part, zz).start()
                        if part == 0 and pairs:
                            cross(b, d, s, zz, False).start()

        def finish(b):
            if pairs:
                for s in range(nz - 1):
                    for d in (1, -1):
                        @pl.when(gets(d, s))
                        def _():
                            cross(b, d, s, z - d * (s + 1), True).wait_recv()

        def give(b):
            src, dst = ((kout, kin), (vout, vin))[b]
            return pltpu.make_async_remote_copy(
                src_ref=src, dst_ref=dst, send_sem=ysend.at[nz + b], recv_sem=yrecv.at[nz + b],
                device_id={"seq": other}, device_id_type=MESH,
            )

        def product(b, first):
            r = slice(0, vrows) if first else slice(vrows, 2 * vrows)
            return jnp.dot(vis[r, :], weights[b][...], preferred_element_type=jnp.float32)

        begin_line(0)
        for zz in range(nz):
            vision_out(zz).start()
        for load in loads[2:]:
            load.start()
        queries()
        for s in range(nz - 1):
            step(0, s)
        begin_line(1)
        finish(0)
        for s in range(nz - 1):
            if s == nz - 2:
                for load in loads[3:]:
                    load.wait()
                for zz in range(nz):
                    vision_out(zz).wait_recv()
                    vision_pass(zz, False).start()
                for zz in range(nz):
                    vision_pass(zz, True).wait_recv()
                kout[...] = product(0, False)
                give(0).start()
                kown[...] = product(0, True)
            step(1, s)
        give(0).wait_recv()
        store_keys(kown[...] + kin[...])
        begin(kv_view, ksend, krecv, 0)
        finish(1)
        vout[...] = product(1, False).astype(vout.dtype)
        give(1).start()
        values = product(1, True)
        give(1).wait_recv()
        vbuf[mine, :] = (values + vin[...].astype(jnp.float32)).astype(jnp.bfloat16)
        begin(kv_view, ksend, krecv, 1)

        def settle():
            for b in range(2):
                give(b).wait_send()
                for s in range(nz - 1):
                    for d in (1, -1):
                        @pl.when(can_send(d, s))
                        def _():
                            for part in range(len(parts)):
                                hop(b, d, s, part, z - d * s).wait_send()

                        if pairs:
                            @pl.when(gets(d, s))
                            def _():
                                cross(b, d, s, z - d * (s + 1), False).wait_send()
            for zz in range(nz):
                vision_out(zz).wait_send()
                vision_pass(zz, False).wait_send()

        return loads[2], settle

    def ring_phase():
        own = pl.ds(pl.multiple_of(me * rows, 16), rows)
        loads = [
            pltpu.make_async_copy(key_ref, wk.at[own], load_sem.at[0]),
            pltpu.make_async_copy(value_ref, wv.at[own], load_sem.at[1]),
            pltpu.make_async_copy(vision_ref, vis, load_sem.at[2]),
            pltpu.make_async_copy(out_w_ref, ow, load_sem.at[3]),
        ]
        for load in loads:
            load.start()
        for target in neighbours.values():
            greet(seq=target)
        greet(head=1 - head)
        if pairs:
            greet(groups=partner)
        pl.semaphore_wait(barrier, 4 if pairs else 3)
        loads[0].wait()
        loads[1].wait()
        shared = (rows * 3 // 10 + 15) // 16 * 16 if pairs else 0
        ringed = rows - shared

        def weight_view(b, owner):
            start = owner * rows
            if pairs:
                start = start + odd * shared
            return weights[b].at[pl.ds(pl.multiple_of(start, 16), ringed)]

        def cross(t, s, received):
            direction, b, _ = streams[t]
            owner = at(-direction * (s + 1))
            which = (1 - odd) if received else odd
            start = owner * rows + which * ringed
            v = weights[b].at[pl.ds(pl.multiple_of(start, 16), shared)]
            return pltpu.make_async_remote_copy(
                src_ref=v, dst_ref=v, send_sem=xsend.at[t, s], recv_sem=xrecv.at[t, s],
                device_id={"groups": partner}, device_id_type=MESH,
            )

        begin(weight_view, wsend, wrecv, 0)
        begin(weight_view, wsend, wrecv, 1)
        queries()
        run(weight_view, wsend, wrecv,
            (lambda t, s: cross(t, s, False).start()) if pairs else None)
        if pairs:
            for t, stream in enumerate(streams):
                for s in range(stream[2]):
                    cross(t, s, True).wait_recv()
        loads[2].wait()
        store_keys(jnp.dot(vis[...], wk[...], preferred_element_type=jnp.float32))
        begin(kv_view, ksend, krecv, 0)
        values = jnp.dot(vis[...], wv[...], preferred_element_type=jnp.float32)
        vbuf[mine, :] = values.astype(jnp.bfloat16)
        begin(kv_view, ksend, krecv, 1)

        def settle():
            drain(weight_view, wsend, wrecv)
            if pairs:
                for t, stream in enumerate(streams):
                    for s in range(stream[2]):
                        cross(t, s, False).wait_send()

        return loads[3], settle

    out_load, settle = (line_phase if folds == 2 else ring_phase)()
    run(kv_view, ksend, krecv)

    total = kbuf.shape[0]
    block = min(total, 2048)
    scale = HEAD_SIZE ** (-0.5)
    attended = (a0, a1)
    mine_text = pl.ds(pl.multiple_of(me * text, 16), text)

    def text_view(b, owner):
        return attended[b].at[pl.ds(pl.multiple_of(owner * text, 16), text)]

    groups_per_buffer = kv_local // 2
    for g in range(kv_local):
        cols = slice(g * HEAD_SIZE, (g + 1) * HEAD_SIZE)
        q = qs[g * per_group * text:(g + 1) * per_group * text, :]
        top = None
        for r in range(0, total, block):
            scores = lax.dot_general(
                q, kbuf[r:r + block, cols], (((1,), (1,)), ((), ())),
                preferred_element_type=jnp.float32,
            ) * scale
            high = jnp.max(scores, axis=-1, keepdims=True)
            new = high if top is None else jnp.maximum(top, high)
            weight = jnp.exp(scores - new)
            part = jnp.sum(weight, axis=-1, keepdims=True)
            product = jnp.dot(
                weight.astype(jnp.bfloat16), vbuf[r:r + block, cols],
                preferred_element_type=jnp.float32,
            )
            if top is None:
                den, num = part, product
            else:
                rescale = jnp.exp(top - new)
                den, num = den * rescale + part, num * rescale + product
            top = new
        result = (num / den).astype(jnp.bfloat16)
        b, inner = g // groups_per_buffer, g % groups_per_buffer
        for h in range(per_group):
            column = (inner * per_group + h) * HEAD_SIZE
            attended[b][mine_text, column:column + HEAD_SIZE] = result[h * text:(h + 1) * text, :]
        if inner == groups_per_buffer - 1:
            begin(text_view, asend, arecv, b)
    run(text_view, asend, arecv)
    out_load.wait()

    out_rows = out_ref.shape[0]
    depth = a0.shape[1]

    def project(which):
        r = pl.ds(pl.multiple_of(which * out_rows, 16), out_rows)
        return jnp.dot(
            a0[r, :], ow[:depth, :], preferred_element_type=jnp.float32
        ) + jnp.dot(a1[r, :], ow[depth:, :], preferred_element_type=jnp.float32)

    pout[...] = project(1 - head).astype(jnp.bfloat16)
    swap = pltpu.make_async_remote_copy(
        src_ref=pout, dst_ref=pin, send_sem=psend, recv_sem=precv,
        device_id={"head": 1 - head}, device_id_type=MESH,
    )
    swap.start()
    projected = project(head)
    swap.wait_recv()
    out_ref[...] = (
        res_ref[...].astype(jnp.float32)
        + jnp.tanh(gate_ref[...]) * (projected + pin[...].astype(jnp.float32))
    ).astype(out_ref.dtype)

    swap.wait_send()
    settle()
    drain(kv_view, ksend, krecv)
    drain(text_view, asend, arecv)


def line_kernel(
    n, cuts, extra, offload,
    q_arg, vision_ref, key_ref, value_ref, out_w_ref, res_arg, qgain_arg, kgain_arg, gate_arg,
    out_ref,
    wk, wv, vis, visx, ow, qout, qall, kacc, vacc, kswap, kswap16, vswap, finals, probs, stats, stat_in,
    own_num, rs_out, rs_in, att, total, pout, pin, q_ref, res_ref, qgain_ref, kgain_ref, gate_ref,
    load_sem, send_sem, recv_sem,
):
    group = lax.axis_index("groups")
    me = lax.axis_index("seq")
    head = lax.axis_index("head")
    z, y = me // 2, me % 2
    odd = group % 2
    side = z // 2
    outer = jnp.logical_or(z == 0, z == 3)
    inner = jnp.logical_not(outer)
    pos = {"e": 3 * side, "m": 1 + side, "M": 2 - side, "E": 3 - 3 * side}
    peers = {
        "x": {"groups": group + 1 - 2 * odd}, "y": {"seq": z * 2 + 1 - y}, "h": {"head": 1 - head},
        "e": {"seq": pos["e"] * 2 + y}, "m": {"seq": pos["m"] * 2 + y}, "M": {"seq": pos["M"] * 2 + y},
    }
    rows, cols = key_ref.shape
    vrows = vision_ref.shape[0]
    text = q_arg.shape[0]
    seen = 2 * vrows
    half_rows = vrows // 2
    padded = wk.shape[0] // 4
    lead = y * (padded - rows)
    chunk = rows // cuts
    split = cuts // 2
    per_group = qall.shape[0]
    tokens = n * text // 2
    wide = per_group * HEAD_SIZE
    bf16, f32 = jnp.bfloat16, jnp.float32
    pieces = 8
    width = wide // pieces
    middle = pieces // 2
    group_heads = per_group // pieces
    weights, sources = (wk, wv), (key_ref, value_ref)
    accs, swaps = (kacc, vacc), (kswap, vswap)
    ids = {"to": {}, "from": {}}
    single = {
        "to": ({"out", "qe", "vx", "up"}, {"mid", "in", "fwd", "qm", "vp", "st", "rs", "ax", "ae", "far"}),
        "from": ({"in", "ae"}, {"out", "mid", "fwd", "qe", "qm", "vx", "vp", "up", "st", "rs", "ax", "far"}),
    }

    def near(rel):
        return "n" if rel in ("e", "m") else rel

    def group_of(way, key):
        kind = key[0]
        if kind == "x":
            return "x", key[1], near(key[2])
        if kind == "s":
            halves = way == "from" and key[1] == 1 and key[2] == 0
            return ("far",) if key[2] else ("s", key[1]) + key[3:] * halves
        if kind == "up":
            return key[:2]
        if kind == "vp":
            return ("vp",)
        if way == "from":
            return ("ay", key[1], key[1] * (key[2] // middle)) if kind == "ay" else key
        if kind in ("out", "mid", "fwd"):
            return key[:2]
        if kind == "in":
            return key[:3]
        return (kind,) if kind in ("yv", "yp", "vx", "rs", "ax", "ae", "ay") else key

    def ident(way, group):
        both, roles = ids[way], single[way]
        role = 1 if group[0] in roles[0] else 2 if group[0] in roles[1] else 0
        if group not in both:
            both[group] = role, sum(1 for r, _ in both.values() if r == role)
        role, i = both[group]
        return i if role == 0 else shared[way] + i

    def copy(key, src, dst, to):
        out, into = (ident(way, group_of(way, key)) for way in ("to", "from"))
        return pltpu.make_async_remote_copy(
            src_ref=src, dst_ref=dst, send_sem=send_sem.at[out], recv_sem=recv_sem.at[into],
            device_id=peers[to], device_id_type=MESH,
        )

    def got(key, dst):
        copy(key, dst, dst, "h").wait_recv()

    def sender(log):
        def send(key, view, to):
            src, dst = view() if callable(view) else view
            copy(key, src, dst, to).start()
            log.setdefault(group_of("to", key), []).append(key)
        return send

    def bulk(group, count):
        kind = group[0]
        if kind in ("x", "out", "mid", "in", "fwd"):
            return weights[group[1]].at[pl.ds(0, count * chunk)]
        if kind in ("yv", "yp"):
            return vis.at[pl.ds(0, count * half_rows), pl.ds(0, padded)]
        if kind in ("vx", "vp"):
            return visx.at[pl.ds(0, count * half_rows)]
        if kind in ("s", "far"):
            return swaps[group[1] if kind == "s" else 1].at[0, 0]
        if kind == "up":
            return kswap16.at[0] if group[1] == 0 else vswap.at[2, 0]
        if kind in ("qe", "qm"):
            return qall.at[:, pl.ds(0, 2 * text if kind == "qe" else tokens)]
        if kind == "ax":
            return att.at[0, pl.ds(0, tokens)]
        return {"q": qout, "st": stat_in, "rs": rs_out, "ae": att.at[0], "ay": att.at[0], "p": pout}[kind]

    def drain(log):
        for group, keys in log.items():
            view = bulk(group, len(keys))
            copy(keys[0], view, view, "h").wait_send()

    shared = {"to": 13, "from": 22}
    outer_log, inner_log, log = {}, {}, {}

    def start_of(j, which):
        return j * chunk + which * (rows - chunk - 2 * chunk * j)

    def slot(b, rel, start, size=chunk):
        return weights[b].at[pl.ds(pl.multiple_of(pos[rel] * padded + lead + start, 16), size)]

    def mine(b, rel, j):
        return slot(b, rel, start_of(j, odd))

    def theirs(b, rel, j):
        return slot(b, rel, start_of(j, 1 - odd))

    def source(b, j):
        return sources[b].at[pl.ds(pl.multiple_of(start_of(j, odd), 16), chunk)]

    def column(yy, zz):
        return pl.ds(pl.multiple_of(zz * 2 * rows + yy * (2 * rows - padded), HEAD_SIZE), padded)

    def block(rel):
        return pl.ds(pl.multiple_of(pos[rel] * padded, HEAD_SIZE), padded)

    def part(which, far):
        return pl.ds(pl.multiple_of(far * vrows + which * half_rows, 16), half_rows)

    def lanes(which):
        return pl.ds(pl.multiple_of(which * HEAD_SIZE, HEAD_SIZE), HEAD_SIZE)

    def piece(c):
        return slice(c * width, (c + 1) * width)

    def span(which):
        return pl.ds(pl.multiple_of(which * tokens, 16), tokens)

    def crossed(b, rel, count):
        got(("x", b, rel, 0), slot(b, rel, 0, count * chunk))

    def vision_send(send, i, rel):
        send(("yv", i), lambda: (vision_ref.at[part(head, 0), column(1 - y, pos[rel])],
                                 vis.at[part(head, 1), block(rel)]), "y")

    def vision_pass(send, i, rel):
        got(("yv", i), vis.at[part(head, 1), block(rel)])
        send(("yp", i), lambda: (vis.at[part(head, 1), block(rel)],) * 2, "h")

    def vision_done(i, rel):
        got(("yp", i), vis.at[part(1 - head, 1), block(rel)])

    def give(send, b, x):
        swap = swaps[b]
        swap[x, 0] = accs[b][x, :, lanes(1 - y)].astype(swap.dtype)
        for k in range(2):
            send(("s", b, x, k), lambda k=k: (swap.at[x, 0, pl.ds(k * vrows, vrows)],
                                              swap.at[x, 1, pl.ds((1 - k) * vrows, vrows)]), "y")

    def half(ref, k):
        return ref.at[pl.ds(k * vrows, vrows)]

    def take(b, x):
        if (b, x) == (1, 0):
            for k in range(2):
                got(("s", b, x, k), half(swaps[b].at[x, 1], 1 - k))
        else:
            got(("s", b, x, 0), swaps[b].at[x, 1])
        return accs[b][x, :, lanes(y)] + swaps[b][x, 1].astype(f32)

    def multiply(b, rel, start):
        part = jnp.dot(vis[:, block(rel)], weights[b][block(rel), :], preferred_element_type=f32)
        accs[b][0] = part if start else accs[b][0] + part

    loads = [
        pltpu.make_async_copy(sources[b], weights[b].at[pl.ds(pl.multiple_of(z * padded + lead, 16), rows)], load_sem.at[b])
        for b in range(2)
    ]
    for zz in range(4):
        loads.append(pltpu.make_async_copy(
            vision_ref.at[:, column(y, zz)], vis.at[:vrows, zz * padded:(zz + 1) * padded],
            load_sem.at[2 + zz]))
    out_load = pltpu.make_async_copy(out_w_ref, ow, load_sem.at[6])
    small = [
        pltpu.make_async_copy(src, dst, load_sem.at[7 + i])
        for i, (src, dst) in enumerate([
            (q_arg, q_ref), (qgain_arg, qgain_ref), (kgain_arg, kgain_ref), (gate_arg, gate_ref), (res_arg, res_ref)])
    ]
    for load in small:
        load.start()

    barrier = pltpu.get_barrier_semaphore()

    def greet(to):
        pl.semaphore_signal(barrier, inc=1, device_id=peers[to], device_id_type=MESH)

    greet("y")
    greet("h")
    greet("x")

    @pl.when(outer)
    def _():
        greet("m")
        pl.semaphore_wait(barrier, 4)

    @pl.when(inner)
    def _():
        greet("e")
        greet("M")
        pl.semaphore_wait(barrier, 5)

    first = split + extra
    order_e = ("E", "e", "m", "M")
    order_m = ("m", "e", "M", "E")
    inward = (("m", "M", "E"), ("m", "M") if offload else ("m", "M", "E"))

    @pl.when(outer)
    def _():
        send = sender(outer_log)
        for j in range(first):
            send(("out", 0, j), lambda j=j: (source(0, j), mine(0, "e", j)), "m")
        vision_send(send, 0, order_e[0])

    @pl.when(inner)
    def _():
        send = sender(inner_log)
        for j in range(split):
            send(("mid", 0, j), lambda j=j: (source(0, j), mine(0, "m", j)), "M")
            send(("in", 0, "m", j), lambda j=j: (source(0, j), mine(0, "m", j)), "e")
        vision_send(send, 0, order_m[0])

    for load in loads:
        load.start()
    out_load.start()
    for w in weights:
        for zz in range(4):
            at = pl.multiple_of(zz * padded + (1 - y) * rows, 16)
            w[pl.ds(at, padded - rows), :] = jnp.zeros((padded - rows, cols), w.dtype)

    for load in small:
        load.wait()
    own_tokens = pl.ds(pl.multiple_of(me * text, 16), text)
    far_tokens = pl.ds(pl.multiple_of((z * 2 + 1 - y) * text, 16), text)
    for h in range(per_group):
        for which in (1 - y, y):
            at = pl.ds(pl.multiple_of(which * wide + h * HEAD_SIZE, HEAD_SIZE), HEAD_SIZE)
            value = norm(q_ref[:, at].astype(f32), qgain_ref[...]).astype(bf16)
            if which is y:
                qall[h, own_tokens, :] = value
            else:
                qout[h] = value
    sender(log)(("q",), lambda: (qout, qall.at[:, own_tokens, :]), "y")

    def line_tokens(zz):
        return qall.at[:, pl.ds(pl.multiple_of(zz * 2 * text, 16), 2 * text), :]

    def side_tokens(which):
        return qall.at[:, span(which), :]

    @pl.when(outer)
    def _():
        send = sender(outer_log)
        for i in range(1, 4):
            vision_send(send, i, order_e[i])

        def inbound(b, rel):
            for j in range(split):
                got(("in", b, rel, j), mine(b, rel, j))
                send(("x", b, rel, j), lambda b=b, rel=rel, j=j: (mine(b, rel, j),) * 2, "x")

        for j in range(first):
            send(("out", 1, j), lambda j=j: (source(1, j), mine(1, "e", j)), "m")
        inbound(0, "m")
        got(("q",), qall.at[:, far_tokens, :])
        send(("qe",), lambda: (line_tokens(z), line_tokens(z)), "m")
        if offload:
            send(("vx", 0), lambda: (vision_ref.at[part(head, 0), column(y, pos["E"])],
                                     visx.at[part(head, 0)]), "m")
        vision_pass(send, 0, "E")
        if offload:
            send(("vx", 1), lambda: (vis.at[part(head, 1), block("E")], visx.at[part(head, 1)]), "m")
        inbound(0, "M")
        vision_pass(send, 1, "e")
        inbound(0, "E")
        vision_pass(send, 2, "m")
        for load in loads:
            load.wait()
        vision_done(1, "e")
        multiply(0, "e", True)
        inbound(1, "m")
        for i, rel in ((0, "E"), (2, "m")):
            vision_done(i, rel)
            crossed(0, rel, split)
            multiply(0, rel, False)
        vision_pass(send, 3, "M")
        for rel in inward[1][1:]:
            inbound(1, rel)
        crossed(0, "M", split)
        vision_done(3, "M")
        multiply(0, "M", False)
        give(send, 0, 0)
        multiply(1, "e", True)
        crossed(1, "m", split)
        multiply(1, "m", False)
        for rel in inward[1][1:]:
            crossed(1, rel, split)
            multiply(1, rel, False)
        give(send, 1, 0)
        kswap16[0] = norm(take(0, 0), kgain_ref[...]).astype(bf16)
        send(("up", 0), lambda: (kswap16.at[0], kswap16.at[1]), "m")
        for k in range(2):
            got(("s", 1, 0, k), half(vswap.at[0, 1], 1 - k))
            here = slice((1 - k) * vrows, (2 - k) * vrows)
            vswap[2, 0, here] = (vacc[0, here, lanes(y)] + vswap[0, 1, here].astype(f32)).astype(bf16)
            send(("up", 1, k), (half(vswap.at[2, 0], 1 - k), half(vswap.at[2, 1], 1 - k)), "m")

    @pl.when(inner)
    def _():
        send = sender(inner_log)
        for i in range(1, 4):
            vision_send(send, i, order_m[i])


        def from_end(b, j):
            got(("out", b, j), mine(b, "e", j))
            if j < split:
                send(("fwd", b, j), lambda: (mine(b, "e", j),) * 2, "M")
            if j < cuts - first:
                send(("x", b, "e", j), lambda: (mine(b, "e", j),) * 2, "x")

        def from_middle(b, j):
            got(("mid", b, j), mine(b, "M", j))
            send(("in", b, "M", j), lambda: (mine(b, "M", j),) * 2, "e")
            send(("x", b, "M", j), lambda: (mine(b, "M", j),) * 2, "x")

        def from_far_end(b, j):
            got(("fwd", b, j), mine(b, "E", j))
            if "E" in inward[b]:
                send(("in", b, "E", j), lambda: (mine(b, "E", j),) * 2, "e")
            send(("x", b, "E", j), lambda: (mine(b, "E", j),) * 2, "x")

        for j in range(first):
            from_end(0, j)
            if j < split:
                from_middle(0, j)
        for j in range(split):
            from_far_end(0, j)
        for j in range(split):
            send(("in", 1, "m", j), lambda j=j: (source(1, j), mine(1, "m", j)), "e")
        vision_pass(send, 0, "m")
        for j in range(first):
            from_end(1, j)
        for j in range(split):
            send(("mid", 1, j), lambda j=j: (source(1, j), mine(1, "m", j)), "M")
        got(("q",), qall.at[:, far_tokens, :])
        vision_pass(send, 1, "e")
        for load in loads:
            load.wait()
        vision_done(0, "m")
        multiply(0, "m", True)
        for j in range(split):
            from_far_end(1, j)
        got(("qe",), line_tokens(pos["e"]))
        send(("qm",), lambda: (side_tokens(side),) * 2, "M")
        for j in range(split):
            from_middle(1, j)
        vision_pass(send, 2, "M")
        vision_done(1, "e")
        crossed(0, "e", cuts - first)
        multiply(0, "e", False)
        vision_done(2, "M")
        crossed(0, "M", split)
        multiply(0, "M", False)
        vision_pass(send, 3, "E")
        crossed(0, "E", split)
        vision_done(3, "E")
        multiply(0, "E", False)
        give(send, 0, 0)
        multiply(1, "m", True)
        crossed(1, "e", cuts - first)
        multiply(1, "e", False)
        crossed(1, "E", split)
        multiply(1, "E", False)
        if offload:
            for k in range(2):
                got(("vx", k), visx.at[part(head, k)])
                send(("vp", k), lambda k=k: (visx.at[part(head, k)],) * 2, "h")
            got(("vp", 0), visx.at[pl.ds(0, vrows)])
            vacc[1] = jnp.dot(visx[...], wv[block("E"), :], preferred_element_type=f32)
            give(send, 1, 1)
        crossed(1, "M", split)
        multiply(1, "M", False)
        give(send, 1, 0)
        got(("qm",), side_tokens(1 - side))

        lane = lax.broadcasted_iota(jnp.int32, (2 * tokens, HEAD_SIZE), 1)
        scale = HEAD_SIZE ** (-0.5)

        def score(r):
            k = finals[0, r * seen:(r + 1) * seen, :]
            tops = jnp.zeros((2 * tokens, HEAD_SIZE), f32)
            dens = jnp.ones((2 * tokens, HEAD_SIZE), f32)
            for h in range(per_group):
                s = lax.dot_general(
                    qall[h], k, (((1,), (1,)), ((), ())), preferred_element_type=f32) * scale
                top = jnp.max(s, axis=-1, keepdims=True)
                p = jnp.exp(s - top)
                den = jnp.sum(p, axis=-1, keepdims=True)
                probs[h, :, r * seen:(r + 1) * seen] = p.astype(bf16)
                tops = jnp.where(lane == h, top, tops)
                dens = jnp.where(lane == h, den, dens)
            stats[r, 0] = tops
            stats[r, 1] = dens

        finals[0, :seen, :] = norm(take(0, 0), kgain_ref[...]).astype(bf16)
        score(0)
        got(("up", 0), kswap16.at[1])
        finals[0, seen:, :] = kswap16[1]
        score(1)

        def merge(top_a, den_a, top_b, den_b):
            top = jnp.maximum(top_a, top_b)
            fa, fb = jnp.exp(top_a - top), jnp.exp(top_b - top)
            return top, fa * den_a + fb * den_b, fa, fb

        top, den, f0, f1 = merge(stats[0, 0], stats[0, 1], stats[1, 0], stats[1, 1])
        stats[0, 0] = f0
        stats[1, 0] = f1
        stats[2, 0] = top
        stats[2, 1] = den
        send(("st",), lambda: (stats.at[2, :, span(1 - side)], stat_in), "M")

        finals[1, :seen, :] = take(1, 0).astype(bf16)
        far_values = take(1, 1) if offload else 0.0
        got(("up", 1), vswap.at[2, 1])
        finals[1, seen:, :] = (far_values + vswap[2, 1].astype(f32)).astype(bf16)
        got(("st",), stat_in)
        _, den, fs, fo = merge(stats[2, 0, span(side), :], stats[2, 1, span(side), :], stat_in[0], stat_in[1])
        inverse = 1.0 / den
        other = fo * inverse
        mine0 = fs * inverse * stats[0, 0, span(side), :]
        mine1 = fs * inverse * stats[1, 0, span(side), :]
        far0, far1 = stats[0, 0, span(1 - side), :], stats[1, 0, span(1 - side), :]

        def numerator(h, which, c0, c1):
            p = probs[h, span(which), :]
            return (c0[:, h:h + 1] * jnp.dot(p[:, :seen], finals[1, :seen, :], preferred_element_type=f32)
                    + c1[:, h:h + 1] * jnp.dot(p[:, seen:], finals[1, seen:, :], preferred_element_type=f32))


        for c in range(pieces):
            for h in range(c * group_heads, (c + 1) * group_heads):
                rs_out[:, h * HEAD_SIZE:(h + 1) * HEAD_SIZE] = numerator(h, 1 - side, far0, far1).astype(bf16)
            send(("rs", c), lambda c=c: (rs_out.at[:, piece(c)], rs_in.at[:, piece(c)]), "M")
        for h in range(per_group):
            own_num[:, h * HEAD_SIZE:(h + 1) * HEAD_SIZE] = numerator(h, side, mine0, mine1)
        for c in range(pieces):
            got(("rs", c), rs_in.at[:, piece(c)])
            for h in range(c * group_heads, (c + 1) * group_heads):
                at = slice(h * HEAD_SIZE, (h + 1) * HEAD_SIZE)
                att[y, span(side), at] = (
                    own_num[:, at] + other[:, h:h + 1] * rs_in[:, at].astype(f32)).astype(bf16)
            here = lambda c=c: (att.at[y, span(side), piece(c)],) * 2
            send(("ax", c), here, "M")
            send(("ae", 0, c), here, "e")
            send(("ay", 0, c), here, "y")

    out_load.wait()

    def forward(t, c):
        view = lambda: (att.at[y, span(side if t == 0 else 1 - side), piece(c)],) * 2

        @pl.when(outer)
        def _():
            got(("ae", t, c), view()[0])
            sender(outer_log)(("ay", t, c), view, "y")

        if t == 1:
            @pl.when(inner)
            def _():
                send = sender(inner_log)
                got(("ax", c), view()[0])
                send(("ae", 1, c), view, "e")
                send(("ay", 1, c), view, "y")

    def project(t, which, start, stop):
        if which is not y:
            got(("ay", t, start), att.at[
                which, span(side if t == 0 else 1 - side), start * width:stop * width])
        depth = (stop - start) * width
        part = jnp.dot(
            att[which, span(side if t == 0 else 1 - side), start * width:stop * width],
            ow[pl.ds(pl.multiple_of(which * wide + start * width, 16), depth), :],
            preferred_element_type=f32)
        total[t] = part if which is y and start == 0 else total[t] + part

    def settle(t):
        which = side if t == 0 else 1 - side

        @pl.when(which != head)
        def _():
            pout[...] = total[t].astype(bf16)
            copy(("p",), pout, pin, "h").start()

    other = 1 - y
    for c in range(pieces):
        forward(0, c)
    project(0, y, 0, pieces)
    for c in range(middle):
        forward(1, c)
    project(0, other, 0, pieces)
    settle(0)
    for c in range(middle, pieces):
        forward(1, c)
    project(1, y, 0, pieces)
    project(1, other, 0, middle)
    project(1, other, middle, pieces)
    settle(1)
    mine_first = side == head
    projected = jnp.where(mine_first, total[0], total[1])
    got(("p",), pin)
    out_ref[...] = (
        res_ref[...].astype(f32)
        + jnp.tanh(gate_ref[...]) * (projected + pin[...].astype(f32))
    ).astype(out_ref.dtype)
    log["p",] = [("p",)]

    @pl.when(outer)
    def _():
        drain(outer_log)

    @pl.when(inner)
    def _():
        drain(inner_log)

    drain(log)
    for way, sem in (("to", send_sem), ("from", recv_sem)):
        counts = [sum(1 for r, _ in ids[way].values() if r == role) for role in range(3)]
        assert counts[0] == shared[way] and sem.shape[0] == counts[0] + max(counts[1:]), (way, counts, sem.shape)


def line_call(n, queries, vision, key_matrix, value_matrix, out_weight, residual):
    rows, columns = key_matrix.shape
    vrows = vision.shape[0]
    text, qcols = queries.shape
    bf16, f32 = jnp.bfloat16, jnp.float32
    padded = -(-rows // HEAD_SIZE) * HEAD_SIZE
    per_group = qcols // HEAD_SIZE // 2
    tokens = n * text // 2
    seen = 2 * vrows
    scratch = [
        pltpu.VMEM((4 * padded, columns), bf16),
        pltpu.VMEM((4 * padded, columns), bf16),
        pltpu.VMEM((seen, 4 * padded), bf16),
        pltpu.VMEM((seen, padded), bf16),
        pltpu.VMEM(out_weight.shape, bf16),
        pltpu.VMEM((per_group, text, HEAD_SIZE), bf16),
        pltpu.VMEM((per_group, 2 * tokens, HEAD_SIZE), bf16),
        pltpu.VMEM((1, seen, columns), f32),
        pltpu.VMEM((2, seen, columns), f32),
        pltpu.VMEM((1, 2, seen, HEAD_SIZE), f32),
        pltpu.VMEM((2, seen, HEAD_SIZE), bf16),
        pltpu.VMEM((3, 2, seen, HEAD_SIZE), bf16),
        pltpu.VMEM((2, 2 * seen, HEAD_SIZE), bf16),
        pltpu.VMEM((per_group, 2 * tokens, 2 * seen), bf16),
        pltpu.VMEM((3, 2, 2 * tokens, HEAD_SIZE), f32),
        pltpu.VMEM((2, tokens, HEAD_SIZE), f32),
        pltpu.VMEM((tokens, qcols // 2), f32),
        pltpu.VMEM((tokens, qcols // 2), bf16),
        pltpu.VMEM((tokens, qcols // 2), bf16),
        pltpu.VMEM((2, 2 * tokens, qcols // 2), bf16),
        pltpu.VMEM((2,) + residual.shape, f32),
        pltpu.VMEM(residual.shape, bf16),
        pltpu.VMEM(residual.shape, bf16),
        pltpu.VMEM(queries.shape, bf16),
        pltpu.VMEM(residual.shape, bf16),
        pltpu.VMEM((1, HEAD_SIZE), f32),
        pltpu.VMEM((1, HEAD_SIZE), f32),
        pltpu.VMEM((1, 1), f32),
        pltpu.SemaphoreType.DMA((12,)),
        pltpu.SemaphoreType.DMA((29,)),
        pltpu.SemaphoreType.DMA((31 + 6 * (10 // 2) + 2 * 1 + 2 * 8,)),
    ]
    return functools.partial(line_kernel, n, 10, 1, True), scratch


def body(n, folds, pairs, queries, vision, key_matrix, value_matrix, out_weight, residual,
         query_norm_gain, key_norm_gain, attn_gate):
    rows, columns = key_matrix.shape
    vrows, width = vision.shape
    text, qcols = queries.shape
    bf16 = jnp.bfloat16
    vmem = pl.BlockSpec(memory_space=pltpu.VMEM)
    hbm = pl.BlockSpec(memory_space=pl.ANY)
    steps = pltpu.SemaphoreType.DMA((4, n // 2))
    hops = pltpu.SemaphoreType.DMA((8, n // 2))
    if folds == 2:
        depth = n // 2 * (-(-rows // HEAD_SIZE) * HEAD_SIZE)
        seen = (2 * vrows, depth)
        part = (vrows, columns)
    else:
        depth = n * rows
        seen = (vrows, width)
        part = (16, HEAD_SIZE)
    middle = (
        folds == 2 and n == 8 and pairs and columns == 2 * HEAD_SIZE
        and rows % 160 == 0 and qcols % (8 * HEAD_SIZE) == 0
    )
    if middle:
        run, scratch = line_call(n, queries, vision, key_matrix, value_matrix, out_weight, residual)
    else:
        run, scratch = functools.partial(kernel, n, folds, pairs), [
            pltpu.VMEM((depth, columns), bf16),
            pltpu.VMEM((depth, columns), bf16),
            pltpu.VMEM(seen, bf16),
            pltpu.VMEM(out_weight.shape, bf16),
            pltpu.VMEM((n * vrows, columns), bf16),
            pltpu.VMEM((n * vrows, columns), bf16),
            pltpu.VMEM((n * text, qcols // 2), bf16),
            pltpu.VMEM((n * text, qcols // 2), bf16),
            pltpu.VMEM((text * qcols // HEAD_SIZE, HEAD_SIZE), bf16),
            pltpu.VMEM(residual.shape, bf16),
            pltpu.VMEM(residual.shape, bf16),
            pltpu.VMEM(part, jnp.float32),
            pltpu.VMEM(part, jnp.float32),
            pltpu.VMEM(part, jnp.float32),
            pltpu.VMEM(part, bf16),
            pltpu.VMEM(part, bf16),
            pltpu.SemaphoreType.DMA((4 + n // 2,)),
            hops, hops, steps, steps, steps, steps, steps, steps,
            pltpu.SemaphoreType.DMA,
            pltpu.SemaphoreType.DMA,
            pltpu.SemaphoreType.DMA((n // 2 + 2,)),
            pltpu.SemaphoreType.DMA((n // 2 + 2,)),
            pltpu.SemaphoreType.DMA((n // 2,)),
            pltpu.SemaphoreType.DMA((n // 2,)),
        ]
    return pl.pallas_call(
        run,
        out_shape=jax.ShapeDtypeStruct(residual.shape, residual.dtype),
        in_specs=[hbm] * 9 if middle else [vmem, hbm, hbm, hbm, hbm, vmem, vmem, vmem, vmem],
        out_specs=vmem,
        scratch_shapes=scratch,
        compiler_params=pltpu.CompilerParams(
            collective_id=0, has_side_effects=True, vmem_limit_bytes=60 * 1024 * 1024
        ),
    )(
        queries, vision, key_matrix, value_matrix, out_weight, residual,
        query_norm_gain.reshape(1, HEAD_SIZE), key_norm_gain.reshape(1, HEAD_SIZE),
        attn_gate.reshape(1, 1),
    )


def solution(mesh):
    in_specs = (
        P(("groups", "seq"), "head"),
        P(("groups", "seq"), None),
        P("seq", "head"),
        P("seq", "head"),
        P("head", "seq"),
        P(("groups", "head"), "seq"),
        P(),
        P(),
        P(),
    )
    out_specs = P(("groups", "head"), "seq")
    n = mesh.shape["seq"]
    pairs = mesh.shape["groups"] % 2 == 0
    local = functools.partial(body, n, ring_columns(mesh), pairs)
    return jax.shard_map(local, mesh=mesh, in_specs=in_specs, out_specs=out_specs, check_vma=False)
```
